32 devices in a mesh: tm: 4 (over x, core), particle: 2 (over y), cell: 4 (over z).
Axes of the slice: x: 2, y: 2, z: 4, core: 2. Of those that a mesh axis runs over, the one named last changes fastest.
Arguments:
- particles: float32 [4, 30, 2048], P('tm', None, 'particle'), may hold values from -50 to 50
- cell_points: float32 [4, 30, 4096], P('tm', None, 'cell'), may hold values from -50 to 50
- cell_counts: int32 [4], replicated, may hold values from 682 to 4096, as said below
- brownian: float32 [4, 30, 2048], P('tm', None, ('particle', 'cell')), may hold values from -6 to 6
Outputs:
- descent_direction: float32 [4, 30, 2048], P('tm', None, ('particle', 'cell'))
- updated_particles: float32 [4, 30, 2048], P('tm', None, ('particle', 'cell'))
The draws below stay inside these ranges and needn't reach their ends.
Inputs may be any that keep to these rules, and one draw needn't show every extreme that they name: `cell_counts`: some time has all 4096 cells observed.
All inputs are finite; a program needn't handle non-finite values.
Results may differ from the reference program's by a relative error of at most 0.0003.
Values sent between devices are 32-bit elements; how exact they have to be, the bound alone decides.
No kernel may reach another device: no remote copies, remote signals or barrier semaphores. Data moves between devices by JAX's collectives and lax.ppermute only.
A program may use at most 64 MiB of HBM per device.

```python
import math
import jax
import jax.numpy as jnp
from jax import lax

DIMS = 30
TIMES = 4
PARTICLES = 2048
CELLS = 4096


def point_cloud(key, salt_value, point_total):
    base_key = jax.random.fold_in(key, salt_value)
    normal_key = jax.random.fold_in(base_key, 1)
    scale_key = jax.random.fold_in(base_key, 2)
    standard = jnp.clip(jax.random.normal(normal_key, (TIMES, DIMS, point_total), jnp.float32), -6.0, 6.0)
    scales = jnp.exp(jax.random.uniform(scale_key, (TIMES, 1, point_total), jnp.float32, 0.0, math.log(4.0)))
    return standard * scales


def draw_particles(key, part):
    return point_cloud(key, 11, PARTICLES)


def draw_cell_points(key, part):
    return point_cloud(key, 23, CELLS)


def draw_cell_counts(key, part):
    first_key = jax.random.fold_in(key, 31)
    second_key = jax.random.fold_in(key, 37)
    sampled = jax.random.randint(first_key, (TIMES,), CELLS // 6, CELLS + 1, dtype=jnp.int32)
    fullest = jax.random.randint(second_key, (), 0, TIMES, dtype=jnp.int32)
    return jnp.where(jnp.arange(TIMES, dtype=jnp.int32) == fullest, CELLS, sampled).astype(jnp.int32)


def block_levels(stream_key, extent, split, least, largest):
    level, own = 1.0, jax.random.fold_in(stream_key, 6)
    for axis_at, parts in split:
        heights = jnp.exp(jax.random.uniform(jax.random.fold_in(own, axis_at), (parts,), jnp.float32, least / len(split), largest / len(split)))
        level = level * jnp.repeat(heights, extent[axis_at] // parts).reshape([-1 if axis == axis_at else 1 for axis in range(len(extent))])
    return level


def centred(own_key, extent, deviation, bound, split=(), held_as=jnp.bfloat16):
    drawn = deviation * jax.random.normal(own_key, extent, jnp.float32)
    if split:
        drawn = drawn * block_levels(own_key, extent, split, -0.22, 0.18)
    return jnp.clip(drawn, -bound, bound).astype(held_as)


def setup_inputs(seed: int = 0) -> dict:
    splits = jax.random.split(jax.random.key(seed), 5)
    particles = draw_particles(jax.random.fold_in(splits[4], 71), 0)
    cell_points = draw_cell_points(jax.random.fold_in(splits[4], 71), 0)
    cell_counts = draw_cell_counts(jax.random.fold_in(splits[4], 71), 0)
    brownian = centred(splits[3], (TIMES, DIMS, PARTICLES), 1.0, 6.0, ((0, 4), (2, 8)), jnp.float32)
    return dict(particles=particles, cell_points=cell_points, cell_counts=cell_counts, brownian=brownian)


DATA_VAR = 2.0
BRIDGE_VAR = 1.5
LANGEVIN_STRIDE = 0.05
NOISE_LEVEL = 1.0

def soft_mean(queries, targets, usable, spread):
    highest = lax.Precision.HIGHEST
    cross_terms = jnp.dot(queries.T, targets, precision=highest, preferred_element_type=jnp.float32)
    scores = (2.0 * cross_terms - lax.optimization_barrier(jnp.sum(queries * queries, 0))[:, None] - lax.optimization_barrier(jnp.sum(targets * targets, 0))[None, :]) / (2.0 * spread)
    scores = jnp.where(usable[None, :], scores, -jnp.inf)
    weights = jax.nn.softmax(scores, axis=1)
    return jnp.dot(targets, weights.T, precision=highest, preferred_element_type=jnp.float32)

def blockwise(queries, targets, usable, spread):
    row_span = math.gcd(queries.shape[1], 512)
    row_pieces = queries.reshape(queries.shape[0], -1, row_span).transpose(1, 0, 2)
    block_means = lax.map(lambda row_piece: soft_mean(row_piece, targets, usable, spread), row_pieces)
    return block_means.transpose(1, 0, 2).reshape(queries.shape)

def reference(particles, cell_points, cell_counts, brownian):
    positions = jnp.arange(CELLS, dtype=jnp.int32)
    everyone = jnp.ones((PARTICLES,), dtype=bool)
    drift_list = []
    moved_list = []
    for time_increment in range(TIMES):
        present_positions = particles[time_increment]
        usable = positions < cell_counts[time_increment]
        fit_mean = blockwise(present_positions, cell_points[time_increment], usable, DATA_VAR)
        gradient = (present_positions - fit_mean) / DATA_VAR
        if time_increment > 0:
            prior_mean = blockwise(present_positions, particles[time_increment - 1], everyone, BRIDGE_VAR)
            gradient = gradient + (present_positions - prior_mean) / BRIDGE_VAR
        if time_increment < TIMES - 1:
            later_mean = blockwise(present_positions, particles[time_increment + 1], everyone, BRIDGE_VAR)
            gradient = gradient + (present_positions - later_mean) / BRIDGE_VAR
        descent_direction = -gradient
        updated_particles = present_positions + LANGEVIN_STRIDE * descent_direction + math.sqrt(2.0 * LANGEVIN_STRIDE * NOISE_LEVEL) * brownian[time_increment]
        drift_list.append(descent_direction)
        moved_list.append(updated_particles)
    return (jnp.stack(drift_list), jnp.stack(moved_list))
```

```python
import functools
import math

import jax
import jax.numpy as jnp
from jax import lax
from jax.experimental import pallas as pl
from jax.experimental.pallas import tpu as pltpu
from jax.sharding import PartitionSpec as P

DATA_VAR = 2.0
BRIDGE_VAR = 1.5
LANGEVIN_STRIDE = 0.05
NOISE_LEVEL = 1.0
LOWEST = -1e30
LANES = 128
GROUP = 32
FIT_SCALE = math.log2(math.e) / DATA_VAR
BRIDGE_SCALE = math.log2(math.e) / BRIDGE_VAR
f32, bf16 = jnp.float32, jnp.bfloat16


def load_columns(ref, features, first, count):
    blocks = ref.shape[0] // features
    return jnp.concatenate(
        [ref[pl.ds(first + k, features, stride=blocks), :] for k in range(count)], 1
    )


def three_parts(x):
    high = x.astype(bf16).astype(f32)
    rest = x - high
    middle = rest.astype(bf16).astype(f32)
    return high, middle, rest - middle


def grouped(x, first, second):
    return jnp.concatenate([x, first, second], 0)


def target_operand(x, scale, usable=None):
    width = x.shape[1]
    zero, one = jnp.zeros((1, width), f32), jnp.ones((1, width), f32)
    norm_high, norm_middle, norm_low = three_parts(-0.5 * scale * jnp.sum(x * x, 0, keepdims=True))
    if usable is not None:
        norm_high = jnp.where(usable, norm_high, LOWEST)
        norm_middle = jnp.where(usable, norm_middle, 0.0)
        norm_low = jnp.where(usable, norm_low, 0.0)
    high, middle, low = three_parts(x)
    return jnp.concatenate(
        [
            grouped(high, norm_high, norm_middle),
            grouped(middle, norm_low, zero),
            grouped(high, one, zero),
            grouped(low, zero, zero),
            grouped(middle, zero, zero),
            grouped(high, zero, zero),
        ],
        0,
    ).astype(bf16)


def query_operand(x, scale):
    width = x.shape[1]
    zero, one = jnp.zeros((1, width), f32), jnp.ones((1, width), f32)
    high, middle, low = three_parts(x * scale)
    return (
        jnp.concatenate(
            [
                grouped(high, one, one),
                grouped(high, one, zero),
                grouped(middle, zero, zero),
                grouped(high, zero, zero),
                grouped(middle, zero, zero),
                grouped(low, zero, zero),
            ],
            0,
        )
        .astype(bf16)
        .T
    )


def partial_sums(queries, targets):
    scores = jnp.dot(queries, targets, preferred_element_type=f32)
    highest = jnp.max(scores, 1, keepdims=True)
    weights = jnp.exp2(scores - highest)
    weights_high = weights.astype(bf16)
    weights_low = (weights - weights_high.astype(f32)).astype(bf16)
    values = targets[2 * GROUP : 5 * GROUP]
    along = (((1,), (1,)), ((), ()))
    sums = lax.dot_general(weights_high, values, along, preferred_element_type=f32)
    sums = sums + lax.dot_general(weights_low, values, along, preferred_element_type=f32)
    column = lax.broadcasted_iota(jnp.int32, sums.shape, 1)
    turned = jnp.where(column == GROUP - 1, highest, sums).T
    return turned[:GROUP] + turned[GROUP : 2 * GROUP] + turned[2 * GROUP : 3 * GROUP]


def merged(parts):
    if len(parts) == 1:
        return parts[0]
    highest = functools.reduce(jnp.maximum, [part[GROUP - 1 :] for part in parts])
    total = sum(part * jnp.exp2(part[GROUP - 1 :] - highest) for part in parts)
    row = lax.broadcasted_iota(jnp.int32, total.shape, 0)
    return jnp.where(row == GROUP - 1, highest, total)


def mean_of(part):
    return part / part[GROUP - 2 : GROUP - 1]


def usable_cells(counts_ref, which, width):
    count = counts_ref[lax.axis_index("tm")]
    position = which * width + lax.broadcasted_iota(jnp.int32, (1, width), 1)
    return position < count


def fit_own(features, halves, counts_ref, block_ref, cells_ref, parts_ref, queries_ref):
    me = lax.axis_index("cell")
    share = parts_ref.shape[2]
    per_share = share // LANES
    columns = [
        load_columns(block_ref, features, lax.bitwise_xor(me, 2 * j) * per_share, per_share)
        for j in range(halves)
    ]
    queries = query_operand(jnp.concatenate(columns, 1), FIT_SCALE)
    queries_ref[...] = queries
    blocks = cells_ref.shape[0] // features
    targets = target_operand(
        load_columns(cells_ref, features, 0, blocks),
        FIT_SCALE,
        usable_cells(counts_ref, me, blocks * LANES),
    )
    parts = partial_sums(queries, targets)
    for j in range(halves):
        parts_ref[j] = parts[:, j * share : (j + 1) * share]


def fit_next(features, halves, counts_ref, queries_ref, cells_ref, parts_ref, *out_refs):
    other = lax.bitwise_xor(lax.axis_index("cell"), 1)
    share = parts_ref.shape[2]
    blocks = cells_ref.shape[0] // features
    targets = target_operand(
        load_columns(cells_ref, features, 0, blocks),
        FIT_SCALE,
        usable_cells(counts_ref, other, blocks * LANES),
    )
    parts = partial_sums(queries_ref[...], targets)
    for j in range(halves):
        out_refs[j][...] = merged([parts_ref[j], parts[:, j * share : (j + 1) * share]])


def bridges(features, sides, block_ref, *refs):
    *key_refs, out_ref = refs
    share = out_ref.shape[1]
    per_share = share // LANES
    x = load_columns(block_ref, features, lax.axis_index("cell") * per_share, per_share)
    queries = query_operand(x, BRIDGE_SCALE)
    time, times = lax.axis_index("tm"), lax.axis_size("tm")
    odd = lax.rem(time, 2)
    pull = jnp.zeros((features, share), f32)
    per_side = len(key_refs) // sides
    for side in range(sides):
        parts = []
        for key_ref in key_refs[side * per_side : (side + 1) * per_side]:
            blocks = key_ref.shape[0] // features
            targets = target_operand(load_columns(key_ref, features, 0, blocks), BRIDGE_SCALE)
            parts.append(partial_sums(queries, targets))
        partner = time + 1 - 2 * odd if side == 0 else time - 1 + 2 * odd
        there = jnp.logical_and(partner >= 0, partner < times)
        mean = mean_of(merged(parts))[:features]
        pull = pull + jnp.where(there, (x - mean) / BRIDGE_VAR, 0.0)
    out_ref[:features, :] = pull


def finish(features, block_ref, noise_ref, pull_ref, *refs):
    *part_refs, drift_ref, moved_ref = refs
    share = pull_ref.shape[1]
    per_share = share // LANES
    first = lax.axis_index("cell") * per_share
    mean = mean_of(merged([ref[...] for ref in part_refs]))
    for k in range(per_share):
        lanes = slice(k * LANES, (k + 1) * LANES)
        rows = pl.ds(k, features, stride=per_share)
        x = block_ref[pl.ds(first + k, features, stride=block_ref.shape[0] // features), :]
        gradient = (x - mean[:features, lanes]) / DATA_VAR + pull_ref[:features, lanes]
        drift = -gradient
        drift_ref[rows, :] = drift
        moved_ref[rows, :] = (
            x
            + LANGEVIN_STRIDE * drift
            + math.sqrt(2.0 * LANGEVIN_STRIDE * NOISE_LEVEL) * noise_ref[rows, :]
        )


VMEM = pl.BlockSpec(memory_space=pltpu.VMEM)
SMEM = pl.BlockSpec(memory_space=pltpu.SMEM)


def call(kernel, out_shape, in_specs, args, flops, out_specs=None):
    out_specs = jax.tree.map(lambda _: VMEM, out_shape) if out_specs is None else out_specs
    return pl.pallas_call(
        kernel,
        out_shape=out_shape,
        in_specs=in_specs,
        out_specs=out_specs,
        compiler_params=pltpu.CompilerParams(vmem_limit_bytes=24 * 1024 * 1024),
        cost_estimate=pl.CostEstimate(
            flops=flops, bytes_accessed=4 * sum(a.size for a in args), transcendentals=0
        ),
    )(*args)


def swaps(mesh_sizes, time_of, particle_shift):
    times, blocks = mesh_sizes
    pairs = []
    for t in range(times):
        if 0 <= time_of(t) < times:
            for p in range(blocks):
                pairs.append((t * blocks + p, time_of(t) * blocks + (p + particle_shift) % blocks))
    return pairs


def shards(particles, cell_points, cell_counts, brownian):
    features = particles.shape[1]
    block = particles.reshape(-1, LANES)
    cells = cell_points.reshape(-1, LANES)
    noise = brownian.reshape(-1, LANES)
    share = brownian.shape[2]
    cell_count, halves = lax.axis_size("cell"), lax.axis_size("cell") // 2
    sizes = (lax.axis_size("tm"), lax.axis_size("particle"))

    def over_cell(x, by):
        return lax.ppermute(x, "cell", [(c, c ^ by) for c in range(cell_count)])

    next_cells = over_cell(cells, 1)
    keys = []
    for time_of in (lambda t: t ^ 1, lambda t: t - 1 if t % 2 == 0 else t + 1):
        for shift in range(sizes[1]):
            keys.append(lax.ppermute(block, ("tm", "particle"), swaps(sizes, time_of, shift)))

    part = jax.ShapeDtypeStruct((GROUP, share), f32)
    parts, queries = call(
        functools.partial(fit_own, features, halves),
        (
            jax.ShapeDtypeStruct((halves, GROUP, share), f32),
            jax.ShapeDtypeStruct((halves * share, 6 * GROUP), bf16),
        ),
        [SMEM, VMEM, VMEM],
        (cell_counts, block, cells),
        10**9,
    )
    own, *others = call(
        functools.partial(fit_next, features, halves),
        (part,) * halves,
        [SMEM, VMEM, VMEM, VMEM],
        (cell_counts, queries, next_cells, parts),
        10**9,
    )
    arrived = [over_cell(other, 2 * (j + 1)) for j, other in enumerate(others)]
    pull = call(
        functools.partial(bridges, features, 2),
        part,
        [VMEM] * (1 + len(keys)),
        (block, *keys),
        3 * 10**9,
    )
    out = jax.ShapeDtypeStruct(noise.shape, f32)
    drift, moved = call(
        functools.partial(finish, features),
        (out, out),
        [VMEM] * (4 + len(arrived)),
        (block, noise, pull, own, *arrived),
        10**6,
        out_specs=(pl.BlockSpec(noise.shape, lambda: (0, 0)),) * 2,
    )
    return drift.reshape(brownian.shape), moved.reshape(brownian.shape)


def solution(mesh):
    in_specs = (
        P("tm", None, "particle"),
        P("tm", None, "cell"),
        P(),
        P("tm", None, ("particle", "cell")),
    )
    out_specs = (P("tm", None, ("particle", "cell")), P("tm", None, ("particle", "cell")))
    return jax.shard_map(shards, mesh=mesh, in_specs=in_specs, out_specs=out_specs, check_vma=False)
```

```python
import functools
import math

import jax
import jax.numpy as jnp
from jax import lax
from jax.experimental import pallas as pl
from jax.experimental.pallas import tpu as pltpu
from jax.sharding import PartitionSpec as P

DATA_VAR = 2.0
BRIDGE_VAR = 1.5
LANGEVIN_STRIDE = 0.05
NOISE_LEVEL = 1.0
LOWEST = -1e30
LANES = 128
GROUP = 32
FIT_SCALE = math.log2(math.e) / DATA_VAR
BRIDGE_SCALE = math.log2(math.e) / BRIDGE_VAR
f32, bf16 = jnp.float32, jnp.bfloat16


def load_columns(ref, features, first, count):
    blocks = ref.shape[0] // features
    return jnp.concatenate(
        [ref[pl.ds(first + k, features, stride=blocks), :] for k in range(count)], 1
    )


def three_parts(x):
    high = x.astype(bf16).astype(f32)
    rest = x - high
    middle = rest.astype(bf16).astype(f32)
    return high, middle, rest - middle


def grouped(x, first, second):
    return jnp.concatenate([x, first, second], 0)


def target_operand(x, scale, usable=None):
    width = x.shape[1]
    zero, one = jnp.zeros((1, width), f32), jnp.ones((1, width), f32)
    norm_high, norm_middle, norm_low = three_parts(-0.5 * scale * jnp.sum(x * x, 0, keepdims=True))
    if usable is not None:
        norm_high = jnp.where(usable, norm_high, LOWEST)
        norm_middle = jnp.where(usable, norm_middle, 0.0)
        norm_low = jnp.where(usable, norm_low, 0.0)
    high, middle, low = three_parts(x)
    return jnp.concatenate(
        [
            grouped(high, norm_high, norm_middle),
            grouped(middle, norm_low, zero),
            grouped(high, one, zero),
            grouped(low, zero, zero),
            grouped(middle, zero, zero),
            grouped(high, zero, zero),
        ],
        0,
    ).astype(bf16)


def query_operand(x, scale):
    width = x.shape[1]
    zero, one = jnp.zeros((1, width), f32), jnp.ones((1, width), f32)
    high, middle, low = three_parts(x * scale)
    return (
        jnp.concatenate(
            [
                grouped(high, one, one),
                grouped(high, one, zero),
                grouped(middle, zero, zero),
                grouped(high, zero, zero),
                grouped(middle, zero, zero),
                grouped(low, zero, zero),
            ],
            0,
        )
        .astype(bf16)
        .T
    )


def partial_sums(queries, targets):
    scores = jnp.dot(queries, targets, preferred_element_type=f32)
    highest = jnp.max(scores, 1, keepdims=True)
    weights = jnp.exp2(scores - highest)
    weights_high = weights.astype(bf16)
    weights_low = (weights - weights_high.astype(f32)).astype(bf16)
    values = targets[2 * GROUP : 5 * GROUP]
    along = (((1,), (1,)), ((), ()))
    sums = lax.dot_general(weights_high, values, along, preferred_element_type=f32)
    sums = sums + lax.dot_general(weights_low, values, along, preferred_element_type=f32)
    column = lax.broadcasted_iota(jnp.int32, sums.shape, 1)
    turned = jnp.where(column == GROUP - 1, highest, sums).T
    return turned[:GROUP] + turned[GROUP : 2 * GROUP] + turned[2 * GROUP : 3 * GROUP]


def merged(parts):
    if len(parts) == 1:
        return parts[0]
    highest = functools.reduce(jnp.maximum, [part[GROUP - 1 :] for part in parts])
    total = sum(part * jnp.exp2(part[GROUP - 1 :] - highest) for part in parts)
    row = lax.broadcasted_iota(jnp.int32, total.shape, 0)
    return jnp.where(row == GROUP - 1, highest, total)


def mean_of(part):
    return part / part[GROUP - 2 : GROUP - 1]


def usable_cells(counts_ref, positions_ref, which):
    count = counts_ref[lax.axis_index("tm")]
    return positions_ref[0:1, :] + which * positions_ref.shape[1] < count


def own_cell():
    return lax.axis_index("cell")


def share_columns(ref, features, which, share):
    blocks = share // LANES
    return load_columns(ref, features, which * blocks, blocks)


def whole(ref, features):
    return load_columns(ref, features, 0, ref.shape[0] // features)


def number_cells(positions_ref):
    positions_ref[...] = lax.broadcasted_iota(jnp.int32, positions_ref.shape, 1)


def fit_first(features, share, counts_ref, positions_ref, block_ref, cells_ref, *refs):
    parts_ref, queries_ref, operand_ref = refs
    columns = [
        share_columns(block_ref, features, lax.bitwise_xor(own_cell(), 2 * (j + 1)), share)
        for j in range(parts_ref.shape[0])
    ]
    queries = query_operand(jnp.concatenate(columns, 1), FIT_SCALE)
    queries_ref[...] = queries
    usable = usable_cells(counts_ref, positions_ref, own_cell())
    targets = target_operand(whole(cells_ref, features), FIT_SCALE, usable)
    operand_ref[...] = targets
    parts = partial_sums(queries, targets)
    for j in range(parts_ref.shape[0]):
        parts_ref[j] = parts[:, j * share : (j + 1) * share]


def fit_second(features, share, counts_ref, positions_ref, queries_ref, parts_ref, *refs):
    cells_ref, operand_ref, *fit_refs = refs
    usable = usable_cells(counts_ref, positions_ref, lax.bitwise_xor(own_cell(), 1))
    targets = target_operand(whole(cells_ref, features), FIT_SCALE, usable)
    operand_ref[...] = targets
    parts = partial_sums(queries_ref[...], targets)
    for j, fit_ref in enumerate(fit_refs):
        fit_ref[...] = merged([parts_ref[j], parts[:, j * share : (j + 1) * share]])


def bridge_others(features, share, blocks, *refs):
    side_refs, other_refs = refs[:2], refs[2 : 1 + blocks]
    operand_refs, pull_refs = refs[1 + blocks : 3 + blocks], refs[3 + blocks :]
    queries = query_operand(
        jnp.concatenate([share_columns(r, features, own_cell(), share) for r in other_refs], 1),
        BRIDGE_SCALE,
    )
    for side, (side_ref, operand_ref) in enumerate(zip(side_refs, operand_refs)):
        targets = target_operand(whole(side_ref, features), BRIDGE_SCALE)
        operand_ref[...] = targets
        parts = partial_sums(queries, targets)
        for j, pull_ref in enumerate(pull_refs):
            pull_ref[side * GROUP : (side + 1) * GROUP, :] = parts[:, j * share : (j + 1) * share]


def for_own(features, share, block_ref, *refs):
    own_ref, near_ref, *side_refs = refs[:4]
    fit_ref, pull_ref = refs[4:]
    x = share_columns(block_ref, features, own_cell(), share)
    queries = query_operand(x, FIT_SCALE)
    fit_ref[...] = merged([partial_sums(queries, ref[...]) for ref in (own_ref, near_ref)])
    queries = query_operand(x, BRIDGE_SCALE)
    for side, side_ref in enumerate(side_refs):
        pull_ref[side * GROUP : (side + 1) * GROUP, :] = partial_sums(queries, side_ref[...])


def finish(features, share, blocks, block_ref, noise_ref, *refs):
    pull_refs, fit_refs = refs[:blocks], refs[blocks:-5]
    drift_out, moved_out, drift_ref, moved_ref, sem = refs[-5:]
    per_share = share // LANES
    first = own_cell() * per_share
    time, times = lax.axis_index("tm"), lax.axis_size("tm")
    step = 1 - 2 * lax.rem(time, 2)
    fit_mean = mean_of(merged([ref[...] for ref in fit_refs]))
    side_means = [
        mean_of(merged([ref[side * GROUP : (side + 1) * GROUP, :] for ref in pull_refs]))
        for side in range(2)
    ]
    partners = [time + step, time - step]
    there = [jnp.logical_and(other >= 0, other < times) for other in partners]
    for k in range(per_share):
        lanes = slice(k * LANES, (k + 1) * LANES)
        x = block_ref[pl.ds(first + k, features, stride=block_ref.shape[0] // features), :]
        gradient = (x - fit_mean[:features, lanes]) / DATA_VAR
        for mean, present in zip(side_means, there):
            gradient = gradient + jnp.where(present, (x - mean[:features, lanes]) / BRIDGE_VAR, 0.0)
        drift = -gradient
        drift_ref[:, 0, lanes] = drift
        moved_ref[:, 0, lanes] = (
            x
            + LANGEVIN_STRIDE * drift
            + math.sqrt(2.0 * LANGEVIN_STRIDE * NOISE_LEVEL) * noise_ref[:, 0, lanes]
        )
    copies = [
        pltpu.make_async_copy(drift_ref, drift_out, sem.at[0]),
        pltpu.make_async_copy(moved_ref, moved_out, sem.at[1]),
    ]
    for copy in copies:
        copy.start()
    for copy in copies:
        copy.wait()


VMEM = pl.BlockSpec(memory_space=pltpu.VMEM)
SMEM = pl.BlockSpec(memory_space=pltpu.SMEM)


def call(kernel, out_shape, args, flops, counts=False, out_spec=VMEM, scratch=()):
    return pl.pallas_call(
        kernel,
        out_shape=out_shape,
        in_specs=[SMEM if counts and k == 0 else VMEM for k in range(len(args))],
        out_specs=jax.tree.map(lambda _: out_spec, out_shape),
        scratch_shapes=scratch,
        compiler_params=pltpu.CompilerParams(vmem_limit_bytes=24 * 1024 * 1024),
        cost_estimate=pl.CostEstimate(
            flops=flops, bytes_accessed=4 * sum(a.size for a in args), transcendentals=0
        ),
    )(*args)


def near_pair(t, times):
    return t + 1 - 2 * (t % 2)


def far_pair(t, times):
    return (t - 1 + 2 * (t % 2)) % times


def shards(particles, cell_points, cell_counts, brownian):
    features = particles.shape[1]
    block = particles.reshape(-1, LANES)
    cells = cell_points.reshape(-1, LANES)
    noise = brownian.transpose(1, 0, 2)
    share = brownian.shape[2]
    cell_size, times, blocks = (lax.axis_size(name) for name in ("cell", "tm", "particle"))
    shares = cell_size // 2
    width = cell_points.shape[2]

    def over_cell(x, by):
        return lax.ppermute(x, "cell", [(c, c ^ by) for c in range(cell_size)])

    def over_time(x, pair):
        return lax.ppermute(x, "tm", [(t, pair(t, times)) for t in range(times)])

    def over_particle(x, by):
        return lax.ppermute(x, "particle", [(p, (p + by) % blocks) for p in range(blocks)])

    near_cells = over_cell(cells, 1)
    others = [over_particle(block, by) for by in range(1, blocks)]
    sides = [over_time(block, pair) for pair in (near_pair, far_pair)]

    part = jax.ShapeDtypeStruct((GROUP, share), f32)
    two_parts = jax.ShapeDtypeStruct((2 * GROUP, share), f32)
    operand = jax.ShapeDtypeStruct((6 * GROUP, width), bf16)
    side_operand = jax.ShapeDtypeStruct((6 * GROUP, particles.shape[2]), bf16)
    positions = call(number_cells, jax.ShapeDtypeStruct((8, width), jnp.int32), (), 10**10)
    parts, fit_queries, own_operand = call(
        functools.partial(fit_first, features, share),
        (
            jax.ShapeDtypeStruct((shares - 1, GROUP, share), f32),
            jax.ShapeDtypeStruct(((shares - 1) * share, 6 * GROUP), bf16),
            operand,
        ),
        (cell_counts, positions, block, cells),
        10**9,
        counts=True,
    )
    near_operand, *sent_fits = call(
        functools.partial(fit_second, features, share),
        (operand,) + (part,) * (shares - 1),
        (cell_counts, positions, fit_queries, parts, near_cells),
        10**9,
        counts=True,
    )
    fits = [over_cell(x, 2 * by) for by, x in zip(range(1, shares), sent_fits)]
    side_operands = call(
        functools.partial(bridge_others, features, share, blocks),
        (side_operand, side_operand) + (two_parts,) * (blocks - 1),
        (*sides, *others),
        10**9,
    )
    pulls = [over_particle(x, -by) for by, x in zip(range(1, blocks), side_operands[2:])]
    own_fit, own_pull = call(
        functools.partial(for_own, features, share),
        (part, two_parts),
        (block, own_operand, near_operand, *side_operands[:2]),
        10**9,
    )
    out = jax.ShapeDtypeStruct(noise.shape, f32)
    drift, moved = call(
        functools.partial(finish, features, share, blocks),
        (out, out),
        (block, noise, own_pull, *pulls, own_fit, *fits),
        10**6,
        out_spec=pl.BlockSpec(memory_space=pltpu.HBM),
        scratch=[
            pltpu.VMEM(noise.shape, f32),
            pltpu.VMEM(noise.shape, f32),
            pltpu.SemaphoreType.DMA((2,)),
        ],
    )
    return drift.transpose(1, 0, 2), moved.transpose(1, 0, 2)


def solution(mesh):
    in_specs = (
        P("tm", None, "particle"),
        P("tm", None, "cell"),
        P(),
        P("tm", None, ("particle", "cell")),
    )
    out_specs = (P("tm", None, ("particle", "cell")), P("tm", None, ("particle", "cell")))
    return jax.shard_map(shards, mesh=mesh, in_specs=in_specs, out_specs=out_specs, check_vma=False)
```

```python
import functools
import math

import jax
import jax.numpy as jnp
from jax import lax
from jax.experimental import pallas as pl
from jax.experimental.pallas import tpu as pltpu
from jax.sharding import PartitionSpec as P


DATA_VAR = 2.0
BRIDGE_VAR = 1.5
LANGEVIN_STRIDE = 0.05
NOISE_LEVEL = 1.0
LOWEST = -1e30
LANES = 128
GROUP = 32
FIT_SCALE = math.log2(math.e) / DATA_VAR
BRIDGE_SCALE = math.log2(math.e) / BRIDGE_VAR
f32, bf16 = jnp.float32, jnp.bfloat16


def load_columns(ref, features, first, count):
    blocks = ref.shape[0] // features
    return jnp.concatenate(
        [ref[pl.ds(first + k, features, stride=blocks), :] for k in range(count)], 1
    )


def three_parts(x):
    high = x.astype(bf16).astype(f32)
    rest = x - high
    middle = rest.astype(bf16).astype(f32)
    return high, middle, rest - middle


def grouped(x, first, second):
    return jnp.concatenate([x, first, second], 0)


def target_operand(x, scale, usable=None):
    width = x.shape[1]
    zero, one = jnp.zeros((1, width), f32), jnp.ones((1, width), f32)
    norm_high, norm_middle, norm_low = three_parts(-0.5 * scale * jnp.sum(x * x, 0, keepdims=True))
    if usable is not None:
        norm_high = jnp.where(usable, norm_high, LOWEST)
        norm_middle = jnp.where(usable, norm_middle, 0.0)
        norm_low = jnp.where(usable, norm_low, 0.0)
    high, middle, low = three_parts(x)
    return jnp.concatenate(
        [
            grouped(high, norm_high, norm_middle),
            grouped(middle, norm_low, zero),
            grouped(high, one, zero),
            grouped(low, zero, zero),
            grouped(middle, zero, zero),
            grouped(high, zero, zero),
        ],
        0,
    ).astype(bf16)


def query_operand(x, scale):
    width = x.shape[1]
    zero, one = jnp.zeros((1, width), f32), jnp.ones((1, width), f32)
    high, middle, low = three_parts(x * scale)
    return (
        jnp.concatenate(
            [
                grouped(high, one, one),
                grouped(high, one, zero),
                grouped(middle, zero, zero),
                grouped(high, zero, zero),
                grouped(middle, zero, zero),
                grouped(low, zero, zero),
            ],
            0,
        )
        .astype(bf16)
        .T
    )


def partial_sums(queries, targets):
    scores = jnp.dot(queries, targets, preferred_element_type=f32)
    highest = jnp.max(scores, 1, keepdims=True)
    weights = jnp.exp2(scores - highest)
    weights_high = weights.astype(bf16)
    weights_low = (weights - weights_high.astype(f32)).astype(bf16)
    values = targets[2 * GROUP : 5 * GROUP]
    along = (((1,), (1,)), ((), ()))
    sums = lax.dot_general(weights_high, values, along, preferred_element_type=f32)
    sums = sums + lax.dot_general(weights_low, values, along, preferred_element_type=f32)
    column = lax.broadcasted_iota(jnp.int32, sums.shape, 1)
    turned = jnp.where(column == GROUP - 1, highest, sums).T
    return turned[:GROUP] + turned[GROUP : 2 * GROUP] + turned[2 * GROUP : 3 * GROUP]


def merged(parts):
    if len(parts) == 1:
        return parts[0]
    highest = functools.reduce(jnp.maximum, [part[GROUP - 1 :] for part in parts])
    total = sum(part * jnp.exp2(part[GROUP - 1 :] - highest) for part in parts)
    row = lax.broadcasted_iota(jnp.int32, total.shape, 0)
    return jnp.where(row == GROUP - 1, highest, total)


def mean_of(part):
    return part / part[GROUP - 2 : GROUP - 1]


def usable_cells(counts_ref, positions_ref, which):
    counts = counts_ref[...].astype(f32)
    here = lax.broadcasted_iota(jnp.int32, counts.shape, 1) == lax.axis_index("tm")
    count = jnp.sum(jnp.where(here, counts, 0.0), 1, keepdims=True).astype(jnp.int32)
    return positions_ref[0:1, :] + which * positions_ref.shape[1] < count


def own_cell():
    return lax.axis_index("cell")


def share_columns(ref, features, which, share):
    blocks = share // LANES
    return load_columns(ref, features, which * blocks, blocks)


def whole(ref, features):
    return load_columns(ref, features, 0, ref.shape[0] // features)


def number_cells(positions_ref):
    positions_ref[...] = lax.broadcasted_iota(jnp.int32, positions_ref.shape, 1)


def fit_first(features, share, counts_ref, positions_ref, block_ref, cells_ref, *refs):
    parts_ref, queries_ref = refs
    columns = [
        share_columns(block_ref, features, lax.bitwise_xor(own_cell(), 2 * j), share)
        for j in range(parts_ref.shape[0])
    ]
    queries = query_operand(jnp.concatenate(columns, 1), FIT_SCALE)
    queries_ref[...] = queries
    usable = usable_cells(counts_ref, positions_ref, own_cell())
    targets = target_operand(whole(cells_ref, features), FIT_SCALE, usable)
    parts = partial_sums(queries, targets)
    for j in range(parts_ref.shape[0]):
        parts_ref[j] = parts[:, j * share : (j + 1) * share]


def fit_second(features, share, counts_ref, positions_ref, queries_ref, parts_ref, *refs):
    cells_ref, operand_ref, *fit_refs = refs
    usable = usable_cells(counts_ref, positions_ref, lax.bitwise_xor(own_cell(), 1))
    targets = target_operand(whole(cells_ref, features), FIT_SCALE, usable)
    operand_ref[...] = targets
    parts = partial_sums(queries_ref[share:, :], targets)
    for j, fit_ref in enumerate(fit_refs):
        fit_ref[...] = merged([parts_ref[j + 1], parts[:, j * share : (j + 1) * share]])


def bridge(queries, key_refs, features):
    targets = [target_operand(whole(ref, features), BRIDGE_SCALE) for ref in key_refs]
    return merged([partial_sums(queries, target) for target in targets])


def own_near(features, share, block_ref, fit_queries_ref, parts_ref, operand_ref, *refs):
    *key_refs, fit_ref, pull_ref, queries_ref = refs
    fit_ref[...] = merged([parts_ref[0], partial_sums(fit_queries_ref[:share, :], operand_ref[...])])
    queries = query_operand(share_columns(block_ref, features, own_cell(), share), BRIDGE_SCALE)
    queries_ref[...] = queries
    pull_ref[...] = bridge(queries, key_refs, features)


def own_far(features, queries_ref, *refs):
    *key_refs, pull_ref = refs
    pull_ref[...] = bridge(queries_ref[...], key_refs, features)


def finish(features, share, block_ref, noise_ref, near_ref, far_ref, *refs):
    fit_refs = refs[:-5]
    drift_out, moved_out, drift_ref, moved_ref, sem = refs[-5:]
    per_share = share // LANES
    first = own_cell() * per_share
    time, times = lax.axis_index("tm"), lax.axis_size("tm")
    step = 1 - 2 * lax.rem(time, 2)
    fit_mean = mean_of(merged([ref[...] for ref in fit_refs]))
    sides = [
        (mean_of(ref[...]), jnp.logical_and(other >= 0, other < times))
        for ref, other in ((near_ref, time + step), (far_ref, time - step))
    ]
    for k in range(per_share):
        lanes = slice(k * LANES, (k + 1) * LANES)
        x = block_ref[pl.ds(first + k, features, stride=block_ref.shape[0] // features), :]
        gradient = (x - fit_mean[:features, lanes]) / DATA_VAR
        for mean, present in sides:
            gradient = gradient + jnp.where(present, (x - mean[:features, lanes]) / BRIDGE_VAR, 0.0)
        drift = -gradient
        drift_ref[:, 0, lanes] = drift
        moved_ref[:, 0, lanes] = (
            x
            + LANGEVIN_STRIDE * drift
            + math.sqrt(2.0 * LANGEVIN_STRIDE * NOISE_LEVEL) * noise_ref[:, 0, lanes]
        )
    copies = [
        pltpu.make_async_copy(drift_ref, drift_out, sem.at[0]),
        pltpu.make_async_copy(moved_ref, moved_out, sem.at[1]),
    ]
    for copy in copies:
        copy.start()
    for copy in copies:
        copy.wait()


VMEM = pl.BlockSpec(memory_space=pltpu.VMEM)


def call(kernel, out_shape, args, flops, out_spec=VMEM, scratch=()):
    return pl.pallas_call(
        kernel,
        out_shape=out_shape,
        in_specs=[VMEM] * len(args),
        out_specs=jax.tree.map(lambda _: out_spec, out_shape),
        scratch_shapes=scratch,
        compiler_params=pltpu.CompilerParams(vmem_limit_bytes=24 * 1024 * 1024),
        cost_estimate=pl.CostEstimate(
            flops=flops, bytes_accessed=4 * sum(a.size for a in args), transcendentals=0
        ),
    )(*args)


def near_pair(t, times):
    return t + 1 - 2 * (t % 2)


def far_pair(t, times):
    return (t - 1 + 2 * (t % 2)) % times


def shards(particles, cell_points, cell_counts, brownian):
    features = particles.shape[1]
    block = particles.reshape(-1, LANES)
    cells = cell_points.reshape(-1, LANES)
    noise = brownian.transpose(1, 0, 2)
    share = brownian.shape[2]
    cell_size, times, blocks = (lax.axis_size(name) for name in ("cell", "tm", "particle"))
    shares = cell_size // 2
    width = cell_points.shape[2]

    def over_cell(x, by):
        return lax.ppermute(x, "cell", [(c, c ^ by) for c in range(cell_size)])

    def over_time(pair, by):
        places = [(t, p) for t in range(times) for p in range(blocks)]
        return lax.ppermute(
            block,
            ("tm", "particle"),
            [(t * blocks + p, pair(t, times) * blocks + (p + by) % blocks) for t, p in places],
        )

    near_cells = over_cell(cells, 1)
    keys = {}
    for side, pair in (("near", near_pair), ("far", far_pair)):
        keys[side] = [over_time(pair, 0)]
        keys[side] += [over_time(pair, by) for by in range(1, blocks)]

    part = jax.ShapeDtypeStruct((GROUP, share), f32)
    operand = jax.ShapeDtypeStruct((6 * GROUP, width), bf16)
    own_queries = jax.ShapeDtypeStruct((share, 6 * GROUP), bf16)
    positions = call(number_cells, jax.ShapeDtypeStruct((8, width), jnp.int32), (), 10**10)
    counts = cell_counts[None]
    parts, fit_queries = call(
        functools.partial(fit_first, features, share),
        (
            jax.ShapeDtypeStruct((shares, GROUP, share), f32),
            jax.ShapeDtypeStruct((shares * share, 6 * GROUP), bf16),
        ),
        (counts, positions, block, cells),
        10**9,
    )
    near_operand, *sent_fits = call(
        functools.partial(fit_second, features, share),
        (operand,) + (part,) * (shares - 1),
        (counts, positions, fit_queries, parts, near_cells),
        10**9,
    )
    fits = [over_cell(x, 2 * by) for by, x in zip(range(1, shares), sent_fits)]
    own_fit, near_pull, bridge_queries = call(
        functools.partial(own_near, features, share),
        (part, part, own_queries),
        (block, fit_queries, parts, near_operand, *keys["near"]),
        10**9,
    )
    far_pull = call(
        functools.partial(own_far, features), part, (bridge_queries, *keys["far"]), 10**9
    )
    out = jax.ShapeDtypeStruct(noise.shape, f32)
    drift, moved = call(
        functools.partial(finish, features, share),
        (out, out),
        (block, noise, near_pull, far_pull, own_fit, *fits),
        10**6,
        out_spec=pl.BlockSpec(memory_space=pltpu.HBM),
        scratch=[
            pltpu.VMEM(noise.shape, f32),
            pltpu.VMEM(noise.shape, f32),
            pltpu.SemaphoreType.DMA((2,)),
        ],
    )
    return drift.transpose(1, 0, 2), moved.transpose(1, 0, 2)


def solution(mesh):
    in_specs = (
        P("tm", None, "particle"),
        P("tm", None, "cell"),
        P(),
        P("tm", None, ("particle", "cell")),
    )
    out_specs = (P("tm", None, ("particle", "cell")), P("tm", None, ("particle", "cell")))
    return jax.shard_map(shards, mesh=mesh, in_specs=in_specs, out_specs=out_specs, check_vma=False)
```

```python
import functools
import math

import jax
import jax.numpy as jnp
from jax import lax
from jax.experimental import pallas as pl
from jax.experimental.pallas import tpu as pltpu
from jax.sharding import PartitionSpec as P


DATA_VAR = 2.0
BRIDGE_VAR = 1.5
LANGEVIN_STRIDE = 0.05
NOISE_LEVEL = 1.0
LOWEST = -1e30
LANES = 128
GROUP = 32
FIT_SCALE = math.log2(math.e) / DATA_VAR
BRIDGE_SCALE = math.log2(math.e) / BRIDGE_VAR
f32, bf16 = jnp.float32, jnp.bfloat16


def load_columns(ref, features, first, count):
    blocks = ref.shape[0] // features
    return jnp.concatenate(
        [ref[pl.ds(first + k, features, stride=blocks), :] for k in range(count)], 1
    )


def three_parts(x):
    high = x.astype(bf16).astype(f32)
    rest = x - high
    middle = rest.astype(bf16).astype(f32)
    return high, middle, rest - middle


def grouped(x, first, second):
    return jnp.concatenate([x, first, second], 0)


def target_operand(x, scale, usable=None):
    width = x.shape[1]
    zero, one = jnp.zeros((1, width), f32), jnp.ones((1, width), f32)
    norm_high, norm_middle, norm_low = three_parts(-0.5 * scale * jnp.sum(x * x, 0, keepdims=True))
    if usable is not None:
        norm_high = jnp.where(usable, norm_high, LOWEST)
        norm_middle = jnp.where(usable, norm_middle, 0.0)
        norm_low = jnp.where(usable, norm_low, 0.0)
    high, middle, low = three_parts(x)
    return jnp.concatenate(
        [
            grouped(high, norm_high, norm_middle),
            grouped(middle, norm_low, zero),
            grouped(high, one, zero),
            grouped(low, zero, zero),
            grouped(middle, zero, zero),
            grouped(high, zero, zero),
        ],
        0,
    ).astype(bf16)


def query_operand(x, scale):
    width = x.shape[1]
    zero, one = jnp.zeros((1, width), f32), jnp.ones((1, width), f32)
    high, middle, low = three_parts(x * scale)
    return (
        jnp.concatenate(
            [
                grouped(high, one, one),
                grouped(high, one, zero),
                grouped(middle, zero, zero),
                grouped(high, zero, zero),
                grouped(middle, zero, zero),
                grouped(low, zero, zero),
            ],
            0,
        )
        .astype(bf16)
        .T
    )


def weigh(scores):
    highest = jnp.max(scores, 1, keepdims=True)
    weights = jnp.exp2(scores - highest)
    weights_high = weights.astype(bf16)
    weights_low = (weights - weights_high.astype(f32)).astype(bf16)
    return highest, weights_high, weights_low


def total(highest, weights_high, weights_low, targets):
    values = targets[2 * GROUP : 5 * GROUP]
    along = (((1,), (1,)), ((), ()))
    sums = lax.dot_general(weights_high, values, along, preferred_element_type=f32)
    sums = sums + lax.dot_general(weights_low, values, along, preferred_element_type=f32)
    column = lax.broadcasted_iota(jnp.int32, sums.shape, 1)
    turned = jnp.where(column == GROUP - 1, highest, sums).T
    return turned[:GROUP] + turned[GROUP : 2 * GROUP] + turned[2 * GROUP : 3 * GROUP]


def many_sums(jobs):
    units = []
    for n, (queries, targets) in enumerate(jobs):
        for first in range(0, queries.shape[0], 256):
            units.append((n, queries[first : first + 256], targets))

    def score(unit):
        return jnp.dot(unit[1], unit[2], preferred_element_type=f32)

    found = [[] for _ in jobs]
    upcoming = score(units[0])
    for k, unit in enumerate(units):
        scores, upcoming = upcoming, score(units[k + 1]) if k + 1 < len(units) else None
        found[unit[0]].append(total(*weigh(scores), unit[2]))
    return [jnp.concatenate(parts, 1) for parts in found]


def partial_sums(queries, targets):
    return many_sums([(queries, targets)])[0]


def merged(parts):
    if len(parts) == 1:
        return parts[0]
    highest = functools.reduce(jnp.maximum, [part[GROUP - 1 :] for part in parts])
    total = sum(part * jnp.exp2(part[GROUP - 1 :] - highest) for part in parts)
    row = lax.broadcasted_iota(jnp.int32, total.shape, 0)
    return jnp.where(row == GROUP - 1, highest, total)


def mean_of(part):
    return part / part[GROUP - 2 : GROUP - 1]


def usable_cells(count, positions_ref, which):
    return positions_ref[0:1, :] + which * positions_ref.shape[1] < count


def own_cell():
    return lax.axis_index("cell")


def share_columns(ref, features, which, share):
    blocks = share // LANES
    return load_columns(ref, features, which * blocks, blocks)


def whole(ref, features):
    return load_columns(ref, features, 0, ref.shape[0] // features)


def number_cells(positions_ref):
    positions_ref[...] = lax.broadcasted_iota(jnp.int32, positions_ref.shape, 1)


def fit_first(features, share, counts_ref, positions_ref, block_ref, cells_ref, *refs):
    parts_ref, queries_ref, count_ref = refs
    columns = [
        share_columns(block_ref, features, lax.bitwise_xor(own_cell(), 2 * j), share)
        for j in range(parts_ref.shape[0])
    ]
    queries = query_operand(jnp.concatenate(columns, 1), FIT_SCALE)
    queries_ref[...] = queries
    counts = counts_ref[...].astype(f32).reshape(1, -1)
    here = lax.broadcasted_iota(jnp.int32, counts.shape, 1) == lax.axis_index("tm")
    count = jnp.sum(jnp.where(here, counts, 0.0), 1, keepdims=True).astype(jnp.int32)
    count_ref[...] = jnp.broadcast_to(count, count_ref.shape)
    usable = usable_cells(count, positions_ref, own_cell())
    targets = target_operand(whole(cells_ref, features), FIT_SCALE, usable)
    parts = partial_sums(queries, targets)
    for j in range(parts_ref.shape[0]):
        parts_ref[j] = parts[:, j * share : (j + 1) * share]


def fit_second(features, share, count_ref, positions_ref, queries_ref, parts_ref, *refs):
    cells_ref, operand_ref, *fit_refs = refs
    usable = usable_cells(count_ref[0:1, 0:1], positions_ref, lax.bitwise_xor(own_cell(), 1))
    targets = target_operand(whole(cells_ref, features), FIT_SCALE, usable)
    operand_ref[...] = targets
    parts = partial_sums(queries_ref[share:, :], targets)
    for j, fit_ref in enumerate(fit_refs):
        fit_ref[...] = merged([parts_ref[j + 1], parts[:, j * share : (j + 1) * share]])


def bridge(queries, key_refs, features):
    targets = [target_operand(whole(ref, features), BRIDGE_SCALE) for ref in key_refs]
    return merged(many_sums([(queries, target) for target in targets]))


def own_near(features, share, block_ref, fit_queries_ref, parts_ref, operand_ref, *refs):
    *key_refs, fit_ref, pull_ref, queries_ref = refs
    fit_ref[...] = merged([parts_ref[0], partial_sums(fit_queries_ref[:share, :], operand_ref[...])])
    queries = query_operand(share_columns(block_ref, features, own_cell(), share), BRIDGE_SCALE)
    queries_ref[...] = queries
    pull_ref[...] = bridge(queries, key_refs, features)


def own_far(features, queries_ref, *refs):
    *key_refs, pull_ref = refs
    pull_ref[...] = bridge(queries_ref[...], key_refs, features)


def finish(features, share, block_ref, noise_ref, near_ref, far_ref, *refs):
    fit_refs = refs[:-5]
    drift_out, moved_out, drift_ref, moved_ref, sem = refs[-5:]
    per_share = share // LANES
    first = own_cell() * per_share
    time, times = lax.axis_index("tm"), lax.axis_size("tm")
    step = 1 - 2 * lax.rem(time, 2)
    fit_mean = mean_of(merged([ref[...] for ref in fit_refs]))
    sides = [
        (mean_of(ref[...]), jnp.logical_and(other >= 0, other < times))
        for ref, other in ((near_ref, time + step), (far_ref, time - step))
    ]
    for k in range(per_share):
        lanes = slice(k * LANES, (k + 1) * LANES)
        x = block_ref[pl.ds(first + k, features, stride=block_ref.shape[0] // features), :]
        gradient = (x - fit_mean[:features, lanes]) / DATA_VAR
        for mean, present in sides:
            gradient = gradient + jnp.where(present, (x - mean[:features, lanes]) / BRIDGE_VAR, 0.0)
        drift = -gradient
        drift_ref[:, 0, lanes] = drift
        moved_ref[:, 0, lanes] = (
            x
            + LANGEVIN_STRIDE * drift
            + math.sqrt(2.0 * LANGEVIN_STRIDE * NOISE_LEVEL) * noise_ref[:, 0, lanes]
        )
    copies = [
        pltpu.make_async_copy(drift_ref, drift_out, sem.at[0]),
        pltpu.make_async_copy(moved_ref, moved_out, sem.at[1]),
    ]
    for copy in copies:
        copy.start()
    for copy in copies:
        copy.wait()


VMEM = pl.BlockSpec(memory_space=pltpu.VMEM)


def call(kernel, out_shape, args, flops, out_spec=VMEM, scratch=()):
    return pl.pallas_call(
        kernel,
        out_shape=out_shape,
        in_specs=[VMEM] * len(args),
        out_specs=jax.tree.map(lambda _: out_spec, out_shape),
        scratch_shapes=scratch,
        compiler_params=pltpu.CompilerParams(vmem_limit_bytes=24 * 1024 * 1024),
        cost_estimate=pl.CostEstimate(
            flops=flops, bytes_accessed=4 * sum(a.size for a in args), transcendentals=0
        ),
    )(*args)


def near_pair(t, times):
    return t + 1 - 2 * (t % 2)


def far_pair(t, times):
    return (t - 1 + 2 * (t % 2)) % times


def shards(particles, cell_points, cell_counts, brownian):
    features = particles.shape[1]
    block = particles.reshape(-1, LANES)
    cells = cell_points.reshape(-1, LANES)
    noise = brownian.transpose(1, 0, 2)
    share = brownian.shape[2]
    cell_size, times, blocks = (lax.axis_size(name) for name in ("cell", "tm", "particle"))
    shares = cell_size // 2
    width = cell_points.shape[2]

    def over_cell(x, by):
        return lax.ppermute(x, "cell", [(c, c ^ by) for c in range(cell_size)])

    def over_time(pair, by):
        places = [(t, p) for t in range(times) for p in range(blocks)]
        return lax.ppermute(
            block,
            ("tm", "particle"),
            [(t * blocks + p, pair(t, times) * blocks + (p + by) % blocks) for t, p in places],
        )

    near_cells = over_cell(cells, 1)
    keys = {}
    for side, pair in (("near", near_pair), ("far", far_pair)):
        keys[side] = [over_time(pair, 0)]
        keys[side] += [over_time(pair, by) for by in range(1, blocks)]

    part = jax.ShapeDtypeStruct((GROUP, share), f32)
    operand = jax.ShapeDtypeStruct((6 * GROUP, width), bf16)
    own_queries = jax.ShapeDtypeStruct((share, 6 * GROUP), bf16)
    positions = call(number_cells, jax.ShapeDtypeStruct((8, width), jnp.int32), (), 10**10)
    parts, fit_queries, count = call(
        functools.partial(fit_first, features, share),
        (
            jax.ShapeDtypeStruct((shares, GROUP, share), f32),
            jax.ShapeDtypeStruct((shares * share, 6 * GROUP), bf16),
            jax.ShapeDtypeStruct((8, LANES), jnp.int32),
        ),
        (cell_counts, positions, block, cells),
        10**9,
    )
    near_operand, *sent_fits = call(
        functools.partial(fit_second, features, share),
        (operand,) + (part,) * (shares - 1),
        (count, positions, fit_queries, parts, near_cells),
        10**9,
    )
    fits = [over_cell(x, 2 * by) for by, x in zip(range(1, shares), sent_fits)]
    own_fit, near_pull, bridge_queries = call(
        functools.partial(own_near, features, share),
        (part, part, own_queries),
        (block, fit_queries, parts, near_operand, *keys["near"]),
        10**9,
    )
    far_pull = call(
        functools.partial(own_far, features), part, (bridge_queries, *keys["far"]), 10**9
    )
    out = jax.ShapeDtypeStruct(noise.shape, f32)
    drift, moved = call(
        functools.partial(finish, features, share),
        (out, out),
        (block, noise, near_pull, far_pull, own_fit, *fits),
        10**6,
        out_spec=pl.BlockSpec(memory_space=pltpu.HBM),
        scratch=[
            pltpu.VMEM(noise.shape, f32),
            pltpu.VMEM(noise.shape, f32),
            pltpu.SemaphoreType.DMA((2,)),
        ],
    )
    return drift.transpose(1, 0, 2), moved.transpose(1, 0, 2)


def solution(mesh):
    in_specs = (
        P("tm", None, "particle"),
        P("tm", None, "cell"),
        P(),
        P("tm", None, ("particle", "cell")),
    )
    out_specs = (P("tm", None, ("particle", "cell")), P("tm", None, ("particle", "cell")))
    return jax.shard_map(shards, mesh=mesh, in_specs=in_specs, out_specs=out_specs, check_vma=False)
```

```python
import functools
import math

import jax
import jax.numpy as jnp
from jax import lax
from jax.experimental import pallas as pl
from jax.experimental.pallas import tpu as pltpu
from jax.sharding import PartitionSpec as P


DATA_VAR = 2.0
BRIDGE_VAR = 1.5
LANGEVIN_STRIDE = 0.05
NOISE_LEVEL = 1.0
LOWEST = -1e30
LANES = 128
GROUP = 32
FIT_SCALE = math.log2(math.e) / DATA_VAR
BRIDGE_SCALE = math.log2(math.e) / BRIDGE_VAR
f32, bf16 = jnp.float32, jnp.bfloat16


def load_columns(ref, features, first, count):
    blocks = ref.shape[0] // features
    return jnp.concatenate(
        [ref[pl.ds(first + k, features, stride=blocks), :] for k in range(count)], 1
    )


def three_parts(x):
    high = x.astype(bf16).astype(f32)
    rest = x - high
    middle = rest.astype(bf16).astype(f32)
    return high, middle, rest - middle


def grouped(x, first, second):
    return jnp.concatenate([x, first, second], 0)


def target_operand(x, scale, usable=None):
    width = x.shape[1]
    zero, one = jnp.zeros((1, width), f32), jnp.ones((1, width), f32)
    norm_high, norm_middle, norm_low = three_parts(-0.5 * scale * jnp.sum(x * x, 0, keepdims=True))
    if usable is not None:
        norm_high = jnp.where(usable, norm_high, LOWEST)
        norm_middle = jnp.where(usable, norm_middle, 0.0)
        norm_low = jnp.where(usable, norm_low, 0.0)
    high, middle, low = three_parts(x)
    return jnp.concatenate(
        [
            grouped(high, norm_high, norm_middle),
            grouped(middle, norm_low, zero),
            grouped(high, one, zero),
            grouped(low, zero, zero),
            grouped(middle, zero, zero),
            grouped(high, zero, zero),
        ],
        0,
    ).astype(bf16)


def query_operand(x, scale):
    width = x.shape[1]
    zero, one = jnp.zeros((1, width), f32), jnp.ones((1, width), f32)
    high, middle, low = three_parts(x * scale)
    return (
        jnp.concatenate(
            [
                grouped(high, one, one),
                grouped(high, one, zero),
                grouped(middle, zero, zero),
                grouped(high, zero, zero),
                grouped(middle, zero, zero),
                grouped(low, zero, zero),
            ],
            0,
        )
        .astype(bf16)
        .T
    )


def weigh(scores):
    highest = jnp.max(scores, 1, keepdims=True)
    weights = jnp.exp2(scores - highest)
    weights_high = weights.astype(bf16)
    weights_low = (weights - weights_high.astype(f32)).astype(bf16)
    return highest, weights_high, weights_low


def total(highest, weights_high, weights_low, targets):
    values = targets[2 * GROUP : 5 * GROUP]
    along = (((1,), (1,)), ((), ()))
    sums = lax.dot_general(weights_high, values, along, preferred_element_type=f32)
    sums = sums + lax.dot_general(weights_low, values, along, preferred_element_type=f32)
    column = lax.broadcasted_iota(jnp.int32, sums.shape, 1)
    turned = jnp.where(column == GROUP - 1, highest, sums).T
    return turned[:GROUP] + turned[GROUP : 2 * GROUP] + turned[2 * GROUP : 3 * GROUP]


def many_sums(jobs, block=256, ahead=1):
    units = []
    for n, (queries, targets) in enumerate(jobs):
        for first in range(0, queries.shape[0], block):
            units.append((n, queries[first : first + block], targets))

    def score(unit):
        return jnp.dot(unit[1], unit[2], preferred_element_type=f32)

    found = [[] for _ in jobs]
    scored = [score(unit) for unit in units[:ahead]]
    for k, unit in enumerate(units):
        if k + ahead < len(units):
            scored.append(score(units[k + ahead]))
        found[unit[0]].append(total(*weigh(scored[k]), unit[2]))
    return [jnp.concatenate(parts, 1) for parts in found]


def partial_sums(queries, targets):
    return many_sums([(queries, targets)])[0]


def merged(parts):
    if len(parts) == 1:
        return parts[0]
    highest = functools.reduce(jnp.maximum, [part[GROUP - 1 :] for part in parts])
    total = sum(part * jnp.exp2(part[GROUP - 1 :] - highest) for part in parts)
    row = lax.broadcasted_iota(jnp.int32, total.shape, 0)
    return jnp.where(row == GROUP - 1, highest, total)


def mean_of(part):
    return part / part[GROUP - 2 : GROUP - 1]


def usable_cells(count, positions_ref, which):
    return positions_ref[0:1, :] + which * positions_ref.shape[1] < count


def own_cell():
    return lax.axis_index("cell")


def share_columns(ref, features, which, share):
    blocks = share // LANES
    return load_columns(ref, features, which * blocks, blocks)


def whole(ref, features):
    return load_columns(ref, features, 0, ref.shape[0] // features)


def number_cells(positions_ref):
    positions_ref[...] = lax.broadcasted_iota(jnp.int32, positions_ref.shape, 1)


def fit_first(features, share, counts_ref, positions_ref, block_ref, cells_ref, *refs):
    parts_ref, queries_ref, count_ref = refs
    columns = [
        share_columns(block_ref, features, lax.bitwise_xor(own_cell(), 2 * j), share)
        for j in range(parts_ref.shape[0])
    ]
    queries = query_operand(jnp.concatenate(columns, 1), FIT_SCALE)
    queries_ref[...] = queries
    counts = counts_ref[...].astype(f32).reshape(1, -1)
    here = lax.broadcasted_iota(jnp.int32, counts.shape, 1) == lax.axis_index("tm")
    count = jnp.sum(jnp.where(here, counts, 0.0), 1, keepdims=True).astype(jnp.int32)
    count_ref[...] = jnp.broadcast_to(count, count_ref.shape)
    usable = usable_cells(count, positions_ref, own_cell())
    targets = target_operand(whole(cells_ref, features), FIT_SCALE, usable)
    parts = partial_sums(queries, targets)
    for j in range(parts_ref.shape[0]):
        parts_ref[j] = parts[:, j * share : (j + 1) * share]


def fit_second(features, share, count_ref, positions_ref, queries_ref, parts_ref, *refs):
    cells_ref, operand_ref, *fit_refs = refs
    usable = usable_cells(count_ref[0:1, 0:1], positions_ref, lax.bitwise_xor(own_cell(), 1))
    targets = target_operand(whole(cells_ref, features), FIT_SCALE, usable)
    operand_ref[...] = targets
    parts = many_sums([(queries_ref[share:, :], targets)], 128, 0)[0]
    for j, fit_ref in enumerate(fit_refs):
        fit_ref[...] = merged([parts_ref[j + 1], parts[:, j * share : (j + 1) * share]])


def bridge(queries, key_refs, features):
    targets = [target_operand(whole(ref, features), BRIDGE_SCALE) for ref in key_refs]
    return merged(many_sums([(queries, target) for target in targets]))


def has_far_side():
    time = lax.axis_index("tm")
    other = time - 1 + 2 * lax.rem(time, 2)
    return jnp.logical_and(other >= 0, other < lax.axis_size("tm"))


def goes_early():
    return jnp.logical_and(own_cell() < lax.axis_size("cell") // 2, has_far_side())


def own_fit(share, queries_ref, parts_ref, operand_ref):
    return merged([parts_ref[0], partial_sums(queries_ref[:share, :], operand_ref[...])])


def own_early(share, queries_ref, parts_ref, operand_ref, fit_ref):
    @pl.when(goes_early())
    def _():
        fit_ref[...] = own_fit(share, queries_ref, parts_ref, operand_ref)

    @pl.when(jnp.logical_not(goes_early()))
    def _():
        fit_ref[...] = jnp.zeros_like(fit_ref)


def own_near(features, share, block_ref, early_ref, fit_queries_ref, parts_ref, operand_ref, *refs):
    *key_refs, fit_ref, pull_ref, queries_ref = refs
    queries = query_operand(share_columns(block_ref, features, own_cell(), share), BRIDGE_SCALE)
    queries_ref[...] = queries

    @pl.when(goes_early())
    def _():
        fit_ref[...] = early_ref[...]
        pull_ref[...] = bridge(queries_ref[...], key_refs, features)

    @pl.when(jnp.logical_not(goes_early()))
    def _():
        fit_ref[...] = own_fit(share, fit_queries_ref, parts_ref, operand_ref)
        pull_ref[...] = bridge(queries_ref[...], key_refs, features)


def own_far(features, queries_ref, *refs):
    *key_refs, pull_ref = refs

    @pl.when(has_far_side())
    def _():
        pull_ref[...] = bridge(queries_ref[...], key_refs, features)

    @pl.when(jnp.logical_not(has_far_side()))
    def _():
        pull_ref[...] = jnp.ones_like(pull_ref)


def finish(features, share, block_ref, noise_ref, near_ref, far_ref, *refs):
    fit_refs = refs[:-5]
    drift_out, moved_out, drift_ref, moved_ref, sem = refs[-5:]
    per_share = share // LANES
    first = own_cell() * per_share
    time, times = lax.axis_index("tm"), lax.axis_size("tm")
    step = 1 - 2 * lax.rem(time, 2)
    fit_mean = mean_of(merged([ref[...] for ref in fit_refs]))
    sides = [
        (mean_of(ref[...]), jnp.logical_and(other >= 0, other < times))
        for ref, other in ((near_ref, time + step), (far_ref, time - step))
    ]
    for k in range(per_share):
        lanes = slice(k * LANES, (k + 1) * LANES)
        x = block_ref[pl.ds(first + k, features, stride=block_ref.shape[0] // features), :]
        gradient = (x - fit_mean[:features, lanes]) / DATA_VAR
        for mean, present in sides:
            gradient = gradient + jnp.where(present, (x - mean[:features, lanes]) / BRIDGE_VAR, 0.0)
        drift = -gradient
        drift_ref[:, 0, lanes] = drift
        moved_ref[:, 0, lanes] = (
            x
            + LANGEVIN_STRIDE * drift
            + math.sqrt(2.0 * LANGEVIN_STRIDE * NOISE_LEVEL) * noise_ref[:, 0, lanes]
        )
    copies = [
        pltpu.make_async_copy(drift_ref, drift_out, sem.at[0]),
        pltpu.make_async_copy(moved_ref, moved_out, sem.at[1]),
    ]
    for copy in copies:
        copy.start()
    for copy in copies:
        copy.wait()


VMEM = pl.BlockSpec(memory_space=pltpu.VMEM)


def call(kernel, out_shape, args, flops, out_spec=VMEM, scratch=()):
    return pl.pallas_call(
        kernel,
        out_shape=out_shape,
        in_specs=[VMEM] * len(args),
        out_specs=jax.tree.map(lambda _: out_spec, out_shape),
        scratch_shapes=scratch,
        compiler_params=pltpu.CompilerParams(vmem_limit_bytes=24 * 1024 * 1024),
        cost_estimate=pl.CostEstimate(
            flops=flops, bytes_accessed=4 * sum(a.size for a in args), transcendentals=0
        ),
    )(*args)


def near_pair(t, times):
    return t + 1 - 2 * (t % 2)


def far_pair(t, times):
    return (t - 1 + 2 * (t % 2)) % times


def shards(particles, cell_points, cell_counts, brownian):
    features = particles.shape[1]
    block = particles.reshape(-1, LANES)
    cells = cell_points.reshape(-1, LANES)
    noise = brownian.transpose(1, 0, 2)
    share = brownian.shape[2]
    cell_size, times, blocks = (lax.axis_size(name) for name in ("cell", "tm", "particle"))
    shares = cell_size // 2
    width = cell_points.shape[2]

    def over_cell(x, by):
        return lax.ppermute(x, "cell", [(c, c ^ by) for c in range(cell_size)])

    def over_time(pair, by):
        places = [(t, p) for t in range(times) for p in range(blocks)]
        return lax.ppermute(
            block,
            ("tm", "particle"),
            [(t * blocks + p, pair(t, times) * blocks + (p + by) % blocks) for t, p in places],
        )

    near_cells = over_cell(cells, 1)
    keys = {}
    for side, pair in (("near", near_pair), ("far", far_pair)):
        keys[side] = [over_time(pair, 0)]
        keys[side] += [over_time(pair, by) for by in range(1, blocks)]

    part = jax.ShapeDtypeStruct((GROUP, share), f32)
    operand = jax.ShapeDtypeStruct((6 * GROUP, width), bf16)
    own_queries = jax.ShapeDtypeStruct((share, 6 * GROUP), bf16)
    positions = call(number_cells, jax.ShapeDtypeStruct((8, width), jnp.int32), (), 10**10)
    parts, fit_queries, count = call(
        functools.partial(fit_first, features, share),
        (
            jax.ShapeDtypeStruct((shares, GROUP, share), f32),
            jax.ShapeDtypeStruct((shares * share, 6 * GROUP), bf16),
            jax.ShapeDtypeStruct((8, LANES), jnp.int32),
        ),
        (cell_counts, positions, block, cells),
        10**9,
    )
    near_operand, *sent_fits = call(
        functools.partial(fit_second, features, share),
        (operand,) + (part,) * (shares - 1),
        (count, positions, fit_queries, parts, near_cells),
        10**9,
    )
    early_fit = call(
        functools.partial(own_early, share), part, (fit_queries, parts, near_operand), 10**9
    )
    fits = [over_cell(x, 2 * by) for by, x in zip(range(1, shares), sent_fits)]
    own_fit, near_pull, bridge_queries = call(
        functools.partial(own_near, features, share),
        (part, part, own_queries),
        (block, early_fit, fit_queries, parts, near_operand, *keys["near"]),
        10**9,
    )
    far_pull = call(
        functools.partial(own_far, features), part, (bridge_queries, *keys["far"]), 10**9
    )
    out = jax.ShapeDtypeStruct(noise.shape, f32)
    drift, moved = call(
        functools.partial(finish, features, share),
        (out, out),
        (block, noise, near_pull, far_pull, own_fit, *fits),
        10**6,
        out_spec=pl.BlockSpec(memory_space=pltpu.HBM),
        scratch=[
            pltpu.VMEM(noise.shape, f32),
            pltpu.VMEM(noise.shape, f32),
            pltpu.SemaphoreType.DMA((2,)),
        ],
    )
    return drift.transpose(1, 0, 2), moved.transpose(1, 0, 2)


def solution(mesh):
    in_specs = (
        P("tm", None, "particle"),
        P("tm", None, "cell"),
        P(),
        P("tm", None, ("particle", "cell")),
    )
    out_specs = (P("tm", None, ("particle", "cell")), P("tm", None, ("particle", "cell")))
    return jax.shard_map(shards, mesh=mesh, in_specs=in_specs, out_specs=out_specs, check_vma=False)
```

```python
import functools
import itertools
import math

import jax
import jax.numpy as jnp
from jax import lax
from jax.experimental import pallas as pl
from jax.experimental.pallas import tpu as pltpu
from jax.sharding import PartitionSpec as P


DATA_VAR = 2.0
BRIDGE_VAR = 1.5
LANGEVIN_STRIDE = 0.05
NOISE_LEVEL = 1.0
LOWEST = -1e30
LANES = 128
GROUP = 32
FIT_SCALE = math.log2(math.e) / DATA_VAR
BRIDGE_SCALE = math.log2(math.e) / BRIDGE_VAR
f32, bf16 = jnp.float32, jnp.bfloat16


def load_columns(ref, features, first, count):
    blocks = ref.shape[0] // features
    return jnp.concatenate(
        [ref[pl.ds(first + k, features, stride=blocks), :] for k in range(count)], 1
    )


def three_parts(x):
    high = x.astype(bf16).astype(f32)
    rest = x - high
    middle = rest.astype(bf16).astype(f32)
    return high, middle, rest - middle


def grouped(x, first, second):
    return jnp.concatenate([x, first, second], 0)


def target_operand(x, scale, usable=None):
    width = x.shape[1]
    zero, one = jnp.zeros((1, width), f32), jnp.ones((1, width), f32)
    norm_high, norm_middle, norm_low = three_parts(-0.5 * scale * jnp.sum(x * x, 0, keepdims=True))
    if usable is not None:
        norm_high = jnp.where(usable, norm_high, LOWEST)
        norm_middle = jnp.where(usable, norm_middle, 0.0)
        norm_low = jnp.where(usable, norm_low, 0.0)
    high, middle, low = three_parts(x)
    return jnp.concatenate(
        [
            grouped(high, norm_high, norm_middle),
            grouped(middle, norm_low, zero),
            grouped(high, one, zero),
            grouped(low, zero, zero),
            grouped(middle, zero, zero),
            grouped(high, zero, zero),
        ],
        0,
    ).astype(bf16)


def query_operand(x, scale):
    width = x.shape[1]
    zero, one = jnp.zeros((1, width), f32), jnp.ones((1, width), f32)
    high, middle, low = three_parts(x * scale)
    return (
        jnp.concatenate(
            [
                grouped(high, one, one),
                grouped(high, one, zero),
                grouped(middle, zero, zero),
                grouped(high, zero, zero),
                grouped(middle, zero, zero),
                grouped(low, zero, zero),
            ],
            0,
        )
        .astype(bf16)
        .T
    )


def weigh(scores):
    highest = jnp.max(scores, 1, keepdims=True)
    weights = jnp.exp2(scores - highest)
    weights_high = weights.astype(bf16)
    weights_low = (weights - weights_high.astype(f32)).astype(bf16)
    return highest, weights_high, weights_low


def total(highest, weights_high, weights_low, targets):
    values = targets[2 * GROUP : 5 * GROUP]
    along = (((1,), (1,)), ((), ()))
    sums = lax.dot_general(weights_high, values, along, preferred_element_type=f32)
    sums = sums + lax.dot_general(weights_low, values, along, preferred_element_type=f32)
    column = lax.broadcasted_iota(jnp.int32, sums.shape, 1)
    turned = jnp.where(column == GROUP - 1, highest, sums).T
    return turned[:GROUP] + turned[GROUP : 2 * GROUP] + turned[2 * GROUP : 3 * GROUP]


def many_sums(jobs, block=128, ahead=3):
    units = []
    for n, (queries, targets) in enumerate(jobs):
        for first in range(0, queries.shape[0], block):
            units.append((n, queries[first : first + block], targets))

    def score(unit):
        return jnp.dot(unit[1], unit[2], preferred_element_type=f32)

    found = [[] for _ in jobs]
    scored = [score(unit) for unit in units[:ahead]]
    for k, unit in enumerate(units):
        if k + ahead < len(units):
            scored.append(score(units[k + ahead]))
        found[unit[0]].append(total(*weigh(scored[k]), unit[2]))
    return [jnp.concatenate(parts, 1) for parts in found]


def merged(parts):
    if len(parts) == 1:
        return parts[0]
    highest = functools.reduce(jnp.maximum, [part[GROUP - 1 :] for part in parts])
    total = sum(part * jnp.exp2(part[GROUP - 1 :] - highest) for part in parts)
    row = lax.broadcasted_iota(jnp.int32, total.shape, 0)
    return jnp.where(row == GROUP - 1, highest, total)


def mean_of(part):
    return part / part[GROUP - 2 : GROUP - 1]


def usable_cells(count, positions_ref, which):
    return positions_ref[0:1, :] + which * positions_ref.shape[1] < count


def own_cell():
    return lax.axis_index("cell")


def share_columns(ref, features, which, share):
    blocks = share // LANES
    return load_columns(ref, features, which * blocks, blocks)


def whole(ref, features):
    return load_columns(ref, features, 0, ref.shape[0] // features)


def number_cells(positions_ref):
    positions_ref[...] = lax.broadcasted_iota(jnp.int32, positions_ref.shape, 1)


def has_far_side():
    time = lax.axis_index("tm")
    other = time - 1 + 2 * lax.rem(time, 2)
    return jnp.logical_and(other >= 0, other < lax.axis_size("tm"))


def lower_half():
    return own_cell() < lax.axis_size("cell") // 2


def either(condition, if_true, if_false):
    pl.when(condition)(if_true)
    pl.when(jnp.logical_not(condition))(if_false)


def fit_queries_of(features, share, block_ref, shares):
    columns = [
        share_columns(block_ref, features, lax.bitwise_xor(own_cell(), 2 * j), share)
        for j in shares
    ]
    return query_operand(jnp.concatenate(columns, 1), FIT_SCALE)


def fit_first(features, share, counts_ref, positions_ref, block_ref, cells_ref, *refs):
    parts_ref, queries_ref, operand_ref, count_ref = refs
    shares = parts_ref.shape[0]

    def for_shares(first):
        queries = fit_queries_of(features, share, block_ref, range(first, shares))
        queries_ref[first * share :, :] = queries
        counts = counts_ref[...].astype(f32).reshape(1, -1)
        here = lax.broadcasted_iota(jnp.int32, counts.shape, 1) == lax.axis_index("tm")
        count = jnp.sum(jnp.where(here, counts, 0.0), 1, keepdims=True).astype(jnp.int32)
        count_ref[...] = jnp.broadcast_to(count, count_ref.shape)
        usable = usable_cells(count, positions_ref, own_cell())
        targets = target_operand(whole(cells_ref, features), FIT_SCALE, usable)
        operand_ref[...] = targets
        block, ahead = (256, 1) if first == 0 else (128, 0)
        parts = many_sums([(queries, targets)], block, ahead)[0]
        for j in range(first, shares):
            at = (j - first) * share
            parts_ref[j] = parts[:, at : at + share]

    def rest():
        parts_ref[0] = jnp.zeros_like(parts_ref[0])
        queries_ref[:share, :] = jnp.zeros((share, queries_ref.shape[1]), bf16)
        for_shares(1)

    either(lower_half(), lambda: for_shares(0), rest)


def fit_early():
    return jnp.logical_and(lower_half(), has_far_side())


def fit_second(features, share, count_ref, positions_ref, queries_ref, parts_ref, *refs):
    cells_ref, operand_ref, own_fit_ref, *fit_refs = refs

    def for_shares(first):
        usable = usable_cells(count_ref[0:1, 0:1], positions_ref, lax.bitwise_xor(own_cell(), 1))
        targets = target_operand(whole(cells_ref, features), FIT_SCALE, usable)
        operand_ref[...] = targets
        block, ahead = (256, 1) if first == 0 else (128, 0)
        parts = many_sums([(queries_ref[first * share :, :], targets)], block, ahead)[0]
        for j, fit_ref in enumerate([own_fit_ref, *fit_refs]):
            if j >= first:
                at = (j - first) * share
                fit_ref[...] = merged([parts_ref[j], parts[:, at : at + share]])

    def rest():
        own_fit_ref[...] = parts_ref[0]
        for_shares(1)

    either(fit_early(), lambda: for_shares(0), rest)


def bridge_queries_of(features, share, block_ref):
    return query_operand(share_columns(block_ref, features, own_cell(), share), BRIDGE_SCALE)


def side_operand(key_ref, features):
    return target_operand(whole(key_ref, features), BRIDGE_SCALE)


def own_near(features, share, block_ref, early_ref, fit_queries_ref, *refs):
    own_ref, near_ref, *key_refs, fit_ref, pull_ref, queries_ref = refs
    queries_ref[...] = bridge_queries_of(features, share, block_ref)

    def pulls(keys, fits):
        queries = queries_ref[...]
        jobs = [(queries, side_operand(key, features)) for key in keys]
        sums = many_sums(fits + jobs)
        return sums[: len(fits)], sums[len(fits) :]

    def early():
        fit_ref[...] = early_ref[...]
        pull_ref[...] = merged(pulls(key_refs, [])[1])

    def early_end():
        fits, sums = pulls(key_refs, [(fit_queries_ref[:share, :], near_ref[...])])
        fit_ref[...] = merged([early_ref[...]] + fits)
        pull_ref[...] = merged(sums)

    def late():
        queries = fit_queries_of(features, share, block_ref, [0])
        fits, sums = pulls(key_refs, [(queries, own_ref[...]), (queries, near_ref[...])])
        fit_ref[...] = merged(fits)
        pull_ref[...] = merged(sums)

    pl.when(fit_early())(early)
    pl.when(jnp.logical_and(lower_half(), jnp.logical_not(has_far_side())))(early_end)
    pl.when(jnp.logical_not(lower_half()))(late)


def bridge(queries, key_refs, features):
    targets = [side_operand(key_ref, features) for key_ref in key_refs]
    return merged(many_sums([(queries, target) for target in targets]))


def own_far(features, queries_ref, *refs):
    *key_refs, pull_ref = refs

    @pl.when(has_far_side())
    def _():
        pull_ref[...] = bridge(queries_ref[...], key_refs, features)

    @pl.when(jnp.logical_not(has_far_side()))
    def _():
        pull_ref[...] = jnp.ones_like(pull_ref)


def finish(features, share, block_ref, noise_ref, near_ref, far_ref, *refs):
    fit_refs = refs[:-5]
    drift_out, moved_out, drift_ref, moved_ref, sem = refs[-5:]
    per_share = share // LANES
    first = own_cell() * per_share
    time, times = lax.axis_index("tm"), lax.axis_size("tm")
    step = 1 - 2 * lax.rem(time, 2)
    fit_mean = mean_of(merged([ref[...] for ref in fit_refs]))
    sides = [
        (mean_of(ref[...]), jnp.logical_and(other >= 0, other < times))
        for ref, other in ((near_ref, time + step), (far_ref, time - step))
    ]
    for k in range(per_share):
        lanes = slice(k * LANES, (k + 1) * LANES)
        x = block_ref[pl.ds(first + k, features, stride=block_ref.shape[0] // features), :]
        gradient = (x - fit_mean[:features, lanes]) / DATA_VAR
        for mean, present in sides:
            gradient = gradient + jnp.where(present, (x - mean[:features, lanes]) / BRIDGE_VAR, 0.0)
        drift = -gradient
        drift_ref[:, 0, lanes] = drift
        moved_ref[:, 0, lanes] = (
            x
            + LANGEVIN_STRIDE * drift
            + math.sqrt(2.0 * LANGEVIN_STRIDE * NOISE_LEVEL) * noise_ref[:, 0, lanes]
        )
    copies = [
        pltpu.make_async_copy(drift_ref, drift_out, sem.at[0]),
        pltpu.make_async_copy(moved_ref, moved_out, sem.at[1]),
    ]
    for copy in copies:
        copy.start()
    for copy in copies:
        copy.wait()


VMEM = pl.BlockSpec(memory_space=pltpu.VMEM)


def call(kernel, out_shape, args, flops, out_spec=VMEM, scratch=()):
    return pl.pallas_call(
        kernel,
        out_shape=out_shape,
        in_specs=[VMEM] * len(args),
        out_specs=jax.tree.map(lambda _: out_spec, out_shape),
        scratch_shapes=scratch,
        compiler_params=pltpu.CompilerParams(vmem_limit_bytes=24 * 1024 * 1024),
        cost_estimate=pl.CostEstimate(
            flops=flops, bytes_accessed=4 * sum(a.size for a in args), transcendentals=0
        ),
    )(*args)


def near_pair(t):
    return t + 1 - 2 * (t % 2)


def far_pair(t):
    return t - 1 + 2 * (t % 2)


def shards(particles, cell_points, cell_counts, brownian):
    features = particles.shape[1]
    block = particles.reshape(-1, LANES)
    cells = cell_points.reshape(-1, LANES)
    noise = brownian.transpose(1, 0, 2)
    share = brownian.shape[2]
    cell_size, times, blocks = (lax.axis_size(name) for name in ("cell", "tm", "particle"))
    shares = cell_size // 2
    width = cell_points.shape[2]

    def over_cell(x, by):
        return lax.ppermute(x, "cell", [(c, c ^ by) for c in range(cell_size)])

    def over_time(pair, by):
        pairs = []
        for t, p, c in itertools.product(range(times), range(blocks), range(cell_size)):
            other, q, d = pair(t), (p + by) % blocks, c
            if not 0 <= other < times:
                other, q, d = (t, p, c ^ 1) if by == 0 else (t, q, c)
            pairs.append(((t * blocks + p) * cell_size + c, (other * blocks + q) * cell_size + d))
        return lax.ppermute(block, ("tm", "particle", "cell"), pairs)

    near_cells = over_cell(cells, 1)
    keys = {}
    for side, pair in (("near", near_pair), ("far", far_pair)):
        keys[side] = [over_time(pair, 0)]
        keys[side] += [over_time(pair, by) for by in range(1, blocks)]

    part = jax.ShapeDtypeStruct((GROUP, share), f32)
    operand = jax.ShapeDtypeStruct((6 * GROUP, width), bf16)
    own_queries = jax.ShapeDtypeStruct((share, 6 * GROUP), bf16)
    positions = call(number_cells, jax.ShapeDtypeStruct((8, width), jnp.int32), (), 10**10)
    parts, fit_queries, own_operand, count = call(
        functools.partial(fit_first, features, share),
        (
            jax.ShapeDtypeStruct((shares, GROUP, share), f32),
            jax.ShapeDtypeStruct((shares * share, 6 * GROUP), bf16),
            operand,
            jax.ShapeDtypeStruct((8, LANES), jnp.int32),
        ),
        (cell_counts, positions, block, cells),
        10**9,
    )
    near_operand, early_fit, *sent_fits = call(
        functools.partial(fit_second, features, share),
        (operand,) + (part,) * shares,
        (count, positions, fit_queries, parts, near_cells),
        10**9,
    )
    fits = [over_cell(x, 2 * by) for by, x in zip(range(1, shares), sent_fits)]
    own_fit, near_pull, bridge_queries = call(
        functools.partial(own_near, features, share),
        (part, part, own_queries),
        (block, early_fit, fit_queries, own_operand, near_operand, *keys["near"]),
        10**9,
    )
    far_pull = call(
        functools.partial(own_far, features), part, (bridge_queries, *keys["far"]), 10**9
    )
    out = jax.ShapeDtypeStruct(noise.shape, f32)
    drift, moved = call(
        functools.partial(finish, features, share),
        (out, out),
        (block, noise, near_pull, far_pull, own_fit, *fits),
        10**6,
        out_spec=pl.BlockSpec(memory_space=pltpu.HBM),
        scratch=[
            pltpu.VMEM(noise.shape, f32),
            pltpu.VMEM(noise.shape, f32),
            pltpu.SemaphoreType.DMA((2,)),
        ],
    )
    return drift.transpose(1, 0, 2), moved.transpose(1, 0, 2)


def solution(mesh):
    in_specs = (
        P("tm", None, "particle"),
        P("tm", None, "cell"),
        P(),
        P("tm", None, ("particle", "cell")),
    )
    out_specs = (P("tm", None, ("particle", "cell")), P("tm", None, ("particle", "cell")))
    return jax.shard_map(shards, mesh=mesh, in_specs=in_specs, out_specs=out_specs, check_vma=False)
```

```python
import functools
import itertools
import math

import jax
import jax.numpy as jnp
from jax import lax
from jax.experimental import pallas as pl
from jax.experimental.pallas import tpu as pltpu
from jax.sharding import PartitionSpec as P


DATA_VAR = 2.0
BRIDGE_VAR = 1.5
LANGEVIN_STRIDE = 0.05
NOISE_LEVEL = 1.0
LOWEST = -1e30
LANES = 128
GROUP = 32
FIT_SCALE = math.log2(math.e) / DATA_VAR
BRIDGE_SCALE = math.log2(math.e) / BRIDGE_VAR
f32, bf16 = jnp.float32, jnp.bfloat16


def load_columns(ref, features, first, count):
    blocks = ref.shape[0] // features
    return jnp.concatenate(
        [ref[pl.ds(first + k, features, stride=blocks), :] for k in range(count)], 1
    )


def three_parts(x):
    high = x.astype(bf16).astype(f32)
    rest = x - high
    middle = rest.astype(bf16).astype(f32)
    return high, middle, rest - middle


def grouped(x, first, second):
    return jnp.concatenate([x, first, second], 0)


def target_operand(x, scale, usable=None):
    width = x.shape[1]
    zero, one = jnp.zeros((1, width), f32), jnp.ones((1, width), f32)
    norm_high, norm_middle, norm_low = three_parts(-0.5 * scale * jnp.sum(x * x, 0, keepdims=True))
    if usable is not None:
        norm_high = jnp.where(usable, norm_high, LOWEST)
        norm_middle = jnp.where(usable, norm_middle, 0.0)
        norm_low = jnp.where(usable, norm_low, 0.0)
    high, middle, low = three_parts(x)
    return jnp.concatenate(
        [
            grouped(high, norm_high, norm_middle),
            grouped(middle, norm_low, zero),
            grouped(high, one, zero),
            grouped(low, zero, zero),
            grouped(middle, zero, zero),
            grouped(high, zero, zero),
        ],
        0,
    ).astype(bf16)


def query_operand(x, scale):
    width = x.shape[1]
    zero, one = jnp.zeros((1, width), f32), jnp.ones((1, width), f32)
    high, middle, low = three_parts(x * scale)
    return (
        jnp.concatenate(
            [
                grouped(high, one, one),
                grouped(high, one, zero),
                grouped(middle, zero, zero),
                grouped(high, zero, zero),
                grouped(middle, zero, zero),
                grouped(low, zero, zero),
            ],
            0,
        )
        .astype(bf16)
        .T
    )


def weigh(scores):
    highest = jnp.max(scores, 1, keepdims=True)
    weights = jnp.exp2(scores - highest)
    weights_high = weights.astype(bf16)
    weights_low = (weights - weights_high.astype(f32)).astype(bf16)
    return highest, weights_high, weights_low


def total(highest, weights_high, weights_low, targets):
    values = targets[2 * GROUP : 5 * GROUP]
    along = (((1,), (1,)), ((), ()))
    sums = lax.dot_general(weights_high, values, along, preferred_element_type=f32)
    sums = sums + lax.dot_general(weights_low, values, along, preferred_element_type=f32)
    column = lax.broadcasted_iota(jnp.int32, sums.shape, 1)
    turned = jnp.where(column == GROUP - 1, highest, sums).T
    return turned[:GROUP] + turned[GROUP : 2 * GROUP] + turned[2 * GROUP : 3 * GROUP]


def many_sums(jobs, block=128, ahead=3):
    units = []
    for n, (queries, targets) in enumerate(jobs):
        for first in range(0, queries.shape[0], block):
            units.append((n, queries[first : first + block], targets))

    def score(unit):
        return jnp.dot(unit[1], unit[2], preferred_element_type=f32)

    found = [[] for _ in jobs]
    scored = [score(unit) for unit in units[:ahead]]
    for k, unit in enumerate(units):
        if k + ahead < len(units):
            scored.append(score(units[k + ahead]))
        found[unit[0]].append(total(*weigh(scored[k]), unit[2]))
    return [jnp.concatenate(parts, 1) for parts in found]


def merged(parts):
    if len(parts) == 1:
        return parts[0]
    highest = functools.reduce(jnp.maximum, [part[GROUP - 1 :] for part in parts])
    total = sum(part * jnp.exp2(part[GROUP - 1 :] - highest) for part in parts)
    row = lax.broadcasted_iota(jnp.int32, total.shape, 0)
    return jnp.where(row == GROUP - 1, highest, total)


def mean_of(part):
    return part / part[GROUP - 2 : GROUP - 1]


def usable_cells(count, positions_ref, which):
    return positions_ref[0:1, :] + which * positions_ref.shape[1] < count


def own_cell():
    return lax.axis_index("cell")


def share_columns(ref, features, which, share):
    blocks = share // LANES
    return load_columns(ref, features, which * blocks, blocks)


def whole(ref, features):
    return load_columns(ref, features, 0, ref.shape[0] // features)


def number_cells(positions_ref):
    positions_ref[...] = lax.broadcasted_iota(jnp.int32, positions_ref.shape, 1)


def has_far_side():
    time = lax.axis_index("tm")
    other = time - 1 + 2 * lax.rem(time, 2)
    return jnp.logical_and(other >= 0, other < lax.axis_size("tm"))


def lower_half():
    return own_cell() < lax.axis_size("cell") // 2


def either(condition, if_true, if_false):
    pl.when(condition)(if_true)
    pl.when(jnp.logical_not(condition))(if_false)


def fit_queries_of(features, share, block_ref, shares):
    columns = [
        share_columns(block_ref, features, lax.bitwise_xor(own_cell(), 2 * j), share)
        for j in shares
    ]
    return query_operand(jnp.concatenate(columns, 1), FIT_SCALE)


def fit_first(features, share, counts_ref, positions_ref, block_ref, cells_ref, *refs):
    parts_ref, queries_ref, operand_ref, count_ref = refs
    shares = parts_ref.shape[0]

    def for_shares(first):
        queries = fit_queries_of(features, share, block_ref, range(first, shares))
        queries_ref[first * share :, :] = queries
        counts = counts_ref[...].astype(f32).reshape(1, -1)
        here = lax.broadcasted_iota(jnp.int32, counts.shape, 1) == lax.axis_index("tm")
        count = jnp.sum(jnp.where(here, counts, 0.0), 1, keepdims=True).astype(jnp.int32)
        count_ref[...] = jnp.broadcast_to(count, count_ref.shape)
        usable = usable_cells(count, positions_ref, own_cell())
        targets = target_operand(whole(cells_ref, features), FIT_SCALE, usable)
        operand_ref[...] = targets
        block, ahead = (128, 3) if first == 0 else (128, 0)
        parts = many_sums([(queries, targets)], block, ahead)[0]
        for j in range(first, shares):
            at = (j - first) * share
            parts_ref[j] = parts[:, at : at + share]

    def rest():
        parts_ref[0] = jnp.zeros_like(parts_ref[0])
        queries_ref[:share, :] = jnp.zeros((share, queries_ref.shape[1]), bf16)
        for_shares(1)

    either(lower_half(), lambda: for_shares(0), rest)


def fit_early():
    odd = lax.rem(lax.axis_index("tm"), 2) == 1
    return jnp.logical_and(odd, jnp.logical_and(lower_half(), has_far_side()))


def fit_second(features, share, count_ref, positions_ref, queries_ref, parts_ref, *refs):
    cells_ref, operand_ref, own_fit_ref, *fit_refs = refs

    def for_shares(first):
        usable = usable_cells(count_ref[0:1, 0:1], positions_ref, lax.bitwise_xor(own_cell(), 1))
        targets = target_operand(whole(cells_ref, features), FIT_SCALE, usable)
        operand_ref[...] = targets
        block, ahead = (128, 3) if first == 0 else (128, 0)
        parts = many_sums([(queries_ref[first * share :, :], targets)], block, ahead)[0]
        for j, fit_ref in enumerate([own_fit_ref, *fit_refs]):
            if j >= first:
                at = (j - first) * share
                fit_ref[...] = merged([parts_ref[j], parts[:, at : at + share]])

    def rest():
        own_fit_ref[...] = parts_ref[0]
        for_shares(1)

    either(fit_early(), lambda: for_shares(0), rest)


def bridge_queries_of(features, share, block_ref):
    return query_operand(share_columns(block_ref, features, own_cell(), share), BRIDGE_SCALE)


def side_operand(key_ref, features):
    return target_operand(whole(key_ref, features), BRIDGE_SCALE)


def own_near(features, share, block_ref, early_ref, fit_queries_ref, *refs):
    own_ref, near_ref, *key_refs, fit_ref, pull_ref, queries_ref = refs
    queries_ref[...] = bridge_queries_of(features, share, block_ref)

    def pulls(keys, fits):
        queries = queries_ref[...]
        jobs = [(queries, side_operand(key, features)) for key in keys]
        sums = many_sums(fits + jobs)
        return sums[: len(fits)], sums[len(fits) :]

    def early():
        fit_ref[...] = early_ref[...]
        pull_ref[...] = merged(pulls(key_refs, [])[1])

    def early_end():
        fits, sums = pulls(key_refs, [(fit_queries_ref[:share, :], near_ref[...])])
        fit_ref[...] = merged([early_ref[...]] + fits)
        pull_ref[...] = merged(sums)

    def late():
        queries = fit_queries_of(features, share, block_ref, [0])
        fits, sums = pulls(key_refs, [(queries, own_ref[...]), (queries, near_ref[...])])
        fit_ref[...] = merged(fits)
        pull_ref[...] = merged(sums)

    pl.when(fit_early())(early)
    pl.when(jnp.logical_and(lower_half(), jnp.logical_not(fit_early())))(early_end)
    pl.when(jnp.logical_not(lower_half()))(late)


def bridge(queries, key_refs, features):
    targets = [side_operand(key_ref, features) for key_ref in key_refs]
    return merged(many_sums([(queries, target) for target in targets]))


def own_far(features, queries_ref, *refs):
    *key_refs, pull_ref = refs

    @pl.when(has_far_side())
    def _():
        pull_ref[...] = bridge(queries_ref[...], key_refs, features)

    @pl.when(jnp.logical_not(has_far_side()))
    def _():
        pull_ref[...] = jnp.ones_like(pull_ref)


def finish(features, share, block_ref, noise_ref, near_ref, far_ref, *refs):
    fit_refs = refs[:-5]
    drift_out, moved_out, drift_ref, moved_ref, sem = refs[-5:]
    per_share = share // LANES
    first = own_cell() * per_share
    time, times = lax.axis_index("tm"), lax.axis_size("tm")
    step = 1 - 2 * lax.rem(time, 2)
    fit_mean = mean_of(merged([ref[...] for ref in fit_refs]))
    sides = [
        (mean_of(ref[...]), jnp.logical_and(other >= 0, other < times))
        for ref, other in ((near_ref, time + step), (far_ref, time - step))
    ]
    for k in range(per_share):
        lanes = slice(k * LANES, (k + 1) * LANES)
        x = block_ref[pl.ds(first + k, features, stride=block_ref.shape[0] // features), :]
        gradient = (x - fit_mean[:features, lanes]) / DATA_VAR
        for mean, present in sides:
            gradient = gradient + jnp.where(present, (x - mean[:features, lanes]) / BRIDGE_VAR, 0.0)
        drift = -gradient
        drift_ref[:, 0, lanes] = drift
        moved_ref[:, 0, lanes] = (
            x
            + LANGEVIN_STRIDE * drift
            + math.sqrt(2.0 * LANGEVIN_STRIDE * NOISE_LEVEL) * noise_ref[:, 0, lanes]
        )
    copies = [
        pltpu.make_async_copy(drift_ref, drift_out, sem.at[0]),
        pltpu.make_async_copy(moved_ref, moved_out, sem.at[1]),
    ]
    for copy in copies:
        copy.start()
    for copy in copies:
        copy.wait()


VMEM = pl.BlockSpec(memory_space=pltpu.VMEM)


def call(kernel, out_shape, args, flops, out_spec=VMEM, scratch=()):
    return pl.pallas_call(
        kernel,
        out_shape=out_shape,
        in_specs=[VMEM] * len(args),
        out_specs=jax.tree.map(lambda _: out_spec, out_shape),
        scratch_shapes=scratch,
        compiler_params=pltpu.CompilerParams(vmem_limit_bytes=24 * 1024 * 1024),
        cost_estimate=pl.CostEstimate(
            flops=flops, bytes_accessed=4 * sum(a.size for a in args), transcendentals=0
        ),
    )(*args)


def near_pair(t):
    return t + 1 - 2 * (t % 2)


def far_pair(t):
    return t - 1 + 2 * (t % 2)


def shards(particles, cell_points, cell_counts, brownian):
    features = particles.shape[1]
    block = particles.reshape(-1, LANES)
    cells = cell_points.reshape(-1, LANES)
    noise = brownian.transpose(1, 0, 2)
    share = brownian.shape[2]
    cell_size, times, blocks = (lax.axis_size(name) for name in ("cell", "tm", "particle"))
    shares = cell_size // 2
    width = cell_points.shape[2]

    def over_cell(x, by):
        return lax.ppermute(x, "cell", [(c, c ^ by) for c in range(cell_size)])

    def over_time(pair, by):
        pairs = []
        for t, p, c in itertools.product(range(times), range(blocks), range(cell_size)):
            other, q, d = pair(t), (p + by) % blocks, c
            if not 0 <= other < times:
                other, q, d = (t, p, c ^ 1) if by == 0 else (t, q, c)
            pairs.append(((t * blocks + p) * cell_size + c, (other * blocks + q) * cell_size + d))
        return lax.ppermute(block, ("tm", "particle", "cell"), pairs)

    near_cells = over_cell(cells, 1)
    keys = {}
    for side, pair in (("near", near_pair), ("far", far_pair)):
        keys[side] = [over_time(pair, 0)]
        keys[side] += [over_time(pair, by) for by in range(1, blocks)]

    part = jax.ShapeDtypeStruct((GROUP, share), f32)
    operand = jax.ShapeDtypeStruct((6 * GROUP, width), bf16)
    own_queries = jax.ShapeDtypeStruct((share, 6 * GROUP), bf16)
    positions = call(number_cells, jax.ShapeDtypeStruct((8, width), jnp.int32), (), 10**10)
    parts, fit_queries, own_operand, count = call(
        functools.partial(fit_first, features, share),
        (
            jax.ShapeDtypeStruct((shares, GROUP, share), f32),
            jax.ShapeDtypeStruct((shares * share, 6 * GROUP), bf16),
            operand,
            jax.ShapeDtypeStruct((8, LANES), jnp.int32),
        ),
        (cell_counts, positions, block, cells),
        10**9,
    )
    near_operand, early_fit, *sent_fits = call(
        functools.partial(fit_second, features, share),
        (operand,) + (part,) * shares,
        (count, positions, fit_queries, parts, near_cells),
        10**9,
    )
    fits = [over_cell(x, 2 * by) for by, x in zip(range(1, shares), sent_fits)]
    own_fit, near_pull, bridge_queries = call(
        functools.partial(own_near, features, share),
        (part, part, own_queries),
        (block, early_fit, fit_queries, own_operand, near_operand, *keys["near"]),
        10**9,
    )
    far_pull = call(
        functools.partial(own_far, features), part, (bridge_queries, *keys["far"]), 10**9
    )
    out = jax.ShapeDtypeStruct(noise.shape, f32)
    drift, moved = call(
        functools.partial(finish, features, share),
        (out, out),
        (block, noise, near_pull, far_pull, own_fit, *fits),
        10**6,
        out_spec=pl.BlockSpec(memory_space=pltpu.HBM),
        scratch=[
            pltpu.VMEM(noise.shape, f32),
            pltpu.VMEM(noise.shape, f32),
            pltpu.SemaphoreType.DMA((2,)),
        ],
    )
    return drift.transpose(1, 0, 2), moved.transpose(1, 0, 2)


def solution(mesh):
    in_specs = (
        P("tm", None, "particle"),
        P("tm", None, "cell"),
        P(),
        P("tm", None, ("particle", "cell")),
    )
    out_specs = (P("tm", None, ("particle", "cell")), P("tm", None, ("particle", "cell")))
    return jax.shard_map(shards, mesh=mesh, in_specs=in_specs, out_specs=out_specs, check_vma=False)
```

```python
import functools
import itertools
import math

import jax
import jax.numpy as jnp
from jax import lax
from jax.experimental import pallas as pl
from jax.experimental.pallas import tpu as pltpu
from jax.sharding import PartitionSpec as P


DATA_VAR = 2.0
BRIDGE_VAR = 1.5
LANGEVIN_STRIDE = 0.05
NOISE_LEVEL = 1.0
LOWEST = -1e30
LANES = 128
GROUP = 32
FIT_SCALE = math.log2(math.e) / DATA_VAR
BRIDGE_SCALE = math.log2(math.e) / BRIDGE_VAR
f32, bf16 = jnp.float32, jnp.bfloat16


def load_columns(ref, features, first, count):
    blocks = ref.shape[0] // features
    return jnp.concatenate(
        [ref[pl.ds(first + k, features, stride=blocks), :] for k in range(count)], 1
    )


def three_parts(x):
    high = x.astype(bf16).astype(f32)
    rest = x - high
    middle = rest.astype(bf16).astype(f32)
    return high, middle, rest - middle


def grouped(x, first, second):
    return jnp.concatenate([x, first, second], 0)


def target_operand(x, scale, usable=None):
    width = x.shape[1]
    zero, one = jnp.zeros((1, width), f32), jnp.ones((1, width), f32)
    norm_high, norm_middle, norm_low = three_parts(-0.5 * scale * jnp.sum(x * x, 0, keepdims=True))
    if usable is not None:
        norm_high = jnp.where(usable, norm_high, LOWEST)
        norm_middle = jnp.where(usable, norm_middle, 0.0)
        norm_low = jnp.where(usable, norm_low, 0.0)
    high, middle, low = three_parts(x)
    return jnp.concatenate(
        [
            grouped(high, norm_high, norm_middle),
            grouped(middle, norm_low, zero),
            grouped(high, one, zero),
            grouped(low, zero, zero),
            grouped(middle, zero, zero),
            grouped(high, zero, zero),
        ],
        0,
    ).astype(bf16)


def query_operand(x, scale):
    width = x.shape[1]
    zero, one = jnp.zeros((1, width), f32), jnp.ones((1, width), f32)
    high, middle, low = three_parts(x * scale)
    return (
        jnp.concatenate(
            [
                grouped(high, one, one),
                grouped(high, one, zero),
                grouped(middle, zero, zero),
                grouped(high, zero, zero),
                grouped(middle, zero, zero),
                grouped(low, zero, zero),
            ],
            0,
        )
        .astype(bf16)
        .T
    )


def weigh(scores):
    highest = jnp.max(scores, 1, keepdims=True)
    weights = jnp.exp2(scores - highest)
    weights_high = weights.astype(bf16)
    weights_low = (weights - weights_high.astype(f32)).astype(bf16)
    return highest, weights_high, weights_low


def total(highest, weights_high, weights_low, targets):
    values = targets[2 * GROUP : 5 * GROUP]
    along = (((1,), (1,)), ((), ()))
    sums = lax.dot_general(weights_high, values, along, preferred_element_type=f32)
    sums = sums + lax.dot_general(weights_low, values, along, preferred_element_type=f32)
    column = lax.broadcasted_iota(jnp.int32, sums.shape, 1)
    turned = jnp.where(column == GROUP - 1, highest, sums).T
    return turned[:GROUP] + turned[GROUP : 2 * GROUP] + turned[2 * GROUP : 3 * GROUP]


def many_sums(jobs, block=128, ahead=3):
    units = []
    for n, (queries, targets) in enumerate(jobs):
        for first in range(0, queries.shape[0], block):
            units.append((n, queries[first : first + block], targets))

    def score(unit):
        return jnp.dot(unit[1], unit[2], preferred_element_type=f32)

    found = [[] for _ in jobs]
    scored = [score(unit) for unit in units[:ahead]]
    for k, unit in enumerate(units):
        if k + ahead < len(units):
            scored.append(score(units[k + ahead]))
        found[unit[0]].append(total(*weigh(scored[k]), unit[2]))
    return [jnp.concatenate(parts, 1) for parts in found]


def merged(parts):
    if len(parts) == 1:
        return parts[0]
    highest = functools.reduce(jnp.maximum, [part[GROUP - 1 :] for part in parts])
    total = sum(part * jnp.exp2(part[GROUP - 1 :] - highest) for part in parts)
    row = lax.broadcasted_iota(jnp.int32, total.shape, 0)
    return jnp.where(row == GROUP - 1, highest, total)


def mean_of(part):
    return part / part[GROUP - 2 : GROUP - 1]


def usable_cells(count, positions_ref, which):
    return positions_ref[0:1, :] + which * positions_ref.shape[1] < count


def own_cell():
    return lax.axis_index("cell")


def share_columns(ref, features, which, share):
    blocks = share // LANES
    return load_columns(ref, features, which * blocks, blocks)


def whole(ref, features):
    return load_columns(ref, features, 0, ref.shape[0] // features)


def number_cells(positions_ref):
    positions_ref[...] = lax.broadcasted_iota(jnp.int32, positions_ref.shape, 1)


def has_far_side():
    time = lax.axis_index("tm")
    other = time - 1 + 2 * lax.rem(time, 2)
    return jnp.logical_and(other >= 0, other < lax.axis_size("tm"))


def lower_half():
    return own_cell() < lax.axis_size("cell") // 2


def either(condition, if_true, if_false):
    pl.when(condition)(if_true)
    pl.when(jnp.logical_not(condition))(if_false)


def fit_queries_of(features, share, block_ref, shares):
    columns = [
        share_columns(block_ref, features, lax.bitwise_xor(own_cell(), 2 * j), share)
        for j in shares
    ]
    return query_operand(jnp.concatenate(columns, 1), FIT_SCALE)


def fit_first(features, share, counts_ref, positions_ref, block_ref, cells_ref, *refs):
    parts_ref, queries_ref, operand_ref, count_ref = refs
    shares = parts_ref.shape[0]

    def for_shares(first):
        queries = fit_queries_of(features, share, block_ref, range(first, shares))
        queries_ref[first * share :, :] = queries
        counts = counts_ref[...].astype(f32).reshape(1, -1)
        here = lax.broadcasted_iota(jnp.int32, counts.shape, 1) == lax.axis_index("tm")
        count = jnp.sum(jnp.where(here, counts, 0.0), 1, keepdims=True).astype(jnp.int32)
        count_ref[...] = jnp.broadcast_to(count, count_ref.shape)
        usable = usable_cells(count, positions_ref, own_cell())
        targets = target_operand(whole(cells_ref, features), FIT_SCALE, usable)
        operand_ref[...] = targets
        block, ahead = (128, 3) if first == 0 else (128, 0)
        parts = many_sums([(queries, targets)], block, ahead)[0]
        for j in range(first, shares):
            at = (j - first) * share
            parts_ref[j] = parts[:, at : at + share]

    def rest():
        parts_ref[0] = jnp.zeros_like(parts_ref[0])
        queries_ref[:share, :] = jnp.zeros((share, queries_ref.shape[1]), bf16)
        for_shares(1)

    either(lower_half(), lambda: for_shares(0), rest)


def fit_early():
    odd = lax.rem(lax.axis_index("tm"), 2) == 1
    return jnp.logical_and(odd, jnp.logical_and(lower_half(), has_far_side()))


def fit_second(features, share, count_ref, positions_ref, queries_ref, parts_ref, *refs):
    cells_ref, operand_ref, own_fit_ref, *fit_refs = refs

    def for_shares(first):
        usable = usable_cells(count_ref[0:1, 0:1], positions_ref, lax.bitwise_xor(own_cell(), 1))
        targets = target_operand(whole(cells_ref, features), FIT_SCALE, usable)
        operand_ref[...] = targets
        block, ahead = (128, 3) if first == 0 else (128, 0)
        parts = many_sums([(queries_ref[first * share :, :], targets)], block, ahead)[0]
        for j, fit_ref in enumerate([own_fit_ref, *fit_refs]):
            if j >= first:
                at = (j - first) * share
                fit_ref[...] = merged([parts_ref[j], parts[:, at : at + share]])

    def rest():
        own_fit_ref[...] = parts_ref[0]
        for_shares(1)

    either(fit_early(), lambda: for_shares(0), rest)


def bridge_queries_of(features, share, block_ref):
    return query_operand(share_columns(block_ref, features, own_cell(), share), BRIDGE_SCALE)


def side_operand(key_ref, features):
    return target_operand(whole(key_ref, features), BRIDGE_SCALE)


def own_near(features, share, block_ref, early_ref, fit_queries_ref, *refs):
    own_ref, near_ref, *key_refs, fit_ref, pull_ref, queries_ref = refs
    queries_ref[...] = bridge_queries_of(features, share, block_ref)

    def pulls(keys, fits):
        queries = queries_ref[...]
        jobs = [(queries, side_operand(key, features)) for key in keys]
        sums = many_sums(fits + jobs)
        return sums[: len(fits)], sums[len(fits) :]

    def early():
        fit_ref[...] = early_ref[...]
        pull_ref[...] = merged(pulls(key_refs, [])[1])

    def early_end():
        fits, sums = pulls(key_refs, [(fit_queries_ref[:share, :], near_ref[...])])
        fit_ref[...] = merged([early_ref[...]] + fits)
        pull_ref[...] = merged(sums)

    def late():
        queries = fit_queries_of(features, share, block_ref, [0])
        fits, sums = pulls(key_refs, [(queries, own_ref[...]), (queries, near_ref[...])])
        fit_ref[...] = merged(fits)
        pull_ref[...] = merged(sums)

    pl.when(fit_early())(early)
    pl.when(jnp.logical_and(lower_half(), jnp.logical_not(fit_early())))(early_end)
    pl.when(jnp.logical_not(lower_half()))(late)


def bridge(queries, key_refs, features):
    targets = [side_operand(key_ref, features) for key_ref in key_refs]
    return merged(many_sums([(queries, target) for target in targets]))


def own_far(features, queries_ref, *refs):
    *key_refs, pull_ref = refs

    @pl.when(has_far_side())
    def _():
        pull_ref[...] = bridge(queries_ref[...], key_refs, features)

    @pl.when(jnp.logical_not(has_far_side()))
    def _():
        pull_ref[...] = jnp.ones_like(pull_ref)


def finish(features, share, block_ref, noise_ref, near_ref, far_ref, *refs):
    fit_refs = refs[:-5]
    drift_out, moved_out, drift_ref, moved_ref, sem = refs[-5:]
    per_share = share // LANES
    first = own_cell() * per_share
    time, times = lax.axis_index("tm"), lax.axis_size("tm")
    step = 1 - 2 * lax.rem(time, 2)
    fit_mean = mean_of(merged([ref[...] for ref in fit_refs]))
    sides = [
        (mean_of(ref[...]), jnp.logical_and(other >= 0, other < times))
        for ref, other in ((near_ref, time + step), (far_ref, time - step))
    ]
    drift_copy = pltpu.make_async_copy(drift_ref, drift_out, sem.at[0])
    moved_copy = pltpu.make_async_copy(moved_ref, moved_out, sem.at[1])
    moves = []
    for k in range(per_share):
        lanes = slice(k * LANES, (k + 1) * LANES)
        x = block_ref[pl.ds(first + k, features, stride=block_ref.shape[0] // features), :]
        gradient = (x - fit_mean[:features, lanes]) / DATA_VAR
        for mean, present in sides:
            gradient = gradient + jnp.where(present, (x - mean[:features, lanes]) / BRIDGE_VAR, 0.0)
        drift = -gradient
        drift_ref[:, 0, lanes] = drift
        moves.append(x + LANGEVIN_STRIDE * drift)
    drift_copy.start()
    for k, move in enumerate(moves):
        lanes = slice(k * LANES, (k + 1) * LANES)
        moved_ref[:, 0, lanes] = (
            move + math.sqrt(2.0 * LANGEVIN_STRIDE * NOISE_LEVEL) * noise_ref[:, 0, lanes]
        )
    moved_copy.start()
    drift_copy.wait()
    moved_copy.wait()


VMEM = pl.BlockSpec(memory_space=pltpu.VMEM)


def call(kernel, out_shape, args, flops, out_spec=VMEM, scratch=()):
    return pl.pallas_call(
        kernel,
        out_shape=out_shape,
        in_specs=[VMEM] * len(args),
        out_specs=jax.tree.map(lambda _: out_spec, out_shape),
        scratch_shapes=scratch,
        compiler_params=pltpu.CompilerParams(vmem_limit_bytes=24 * 1024 * 1024),
        cost_estimate=pl.CostEstimate(
            flops=flops, bytes_accessed=4 * sum(a.size for a in args), transcendentals=0
        ),
    )(*args)


def near_pair(t):
    return t + 1 - 2 * (t % 2)


def far_pair(t):
    return t - 1 + 2 * (t % 2)


def shards(particles, cell_points, cell_counts, brownian):
    features = particles.shape[1]
    block = particles.reshape(-1, LANES)
    cells = cell_points.reshape(-1, LANES)
    noise = brownian.transpose(1, 0, 2)
    share = brownian.shape[2]
    cell_size, times, blocks = (lax.axis_size(name) for name in ("cell", "tm", "particle"))
    shares = cell_size // 2
    width = cell_points.shape[2]

    def over_cell(x, by):
        return lax.ppermute(x, "cell", [(c, c ^ by) for c in range(cell_size)])

    def over_time(pair, by):
        pairs = []
        for t, p, c in itertools.product(range(times), range(blocks), range(cell_size)):
            other, q, d = pair(t), (p + by) % blocks, c
            if not 0 <= other < times:
                other, q, d = (t, p, c ^ 1) if by == 0 else (t, q, c)
            pairs.append(((t * blocks + p) * cell_size + c, (other * blocks + q) * cell_size + d))
        return lax.ppermute(block, ("tm", "particle", "cell"), pairs)

    near_cells = over_cell(cells, 1)
    keys = {}
    for side, pair in (("near", near_pair), ("far", far_pair)):
        keys[side] = [over_time(pair, 0)]
        keys[side] += [over_time(pair, by) for by in range(1, blocks)]

    part = jax.ShapeDtypeStruct((GROUP, share), f32)
    operand = jax.ShapeDtypeStruct((6 * GROUP, width), bf16)
    own_queries = jax.ShapeDtypeStruct((share, 6 * GROUP), bf16)
    positions = call(number_cells, jax.ShapeDtypeStruct((8, width), jnp.int32), (), 10**10)
    parts, fit_queries, own_operand, count = call(
        functools.partial(fit_first, features, share),
        (
            jax.ShapeDtypeStruct((shares, GROUP, share), f32),
            jax.ShapeDtypeStruct((shares * share, 6 * GROUP), bf16),
            operand,
            jax.ShapeDtypeStruct((8, LANES), jnp.int32),
        ),
        (cell_counts, positions, block, cells),
        10**9,
    )
    near_operand, early_fit, *sent_fits = call(
        functools.partial(fit_second, features, share),
        (operand,) + (part,) * shares,
        (count, positions, fit_queries, parts, near_cells),
        10**9,
    )
    fits = [over_cell(x, 2 * by) for by, x in zip(range(1, shares), sent_fits)]
    own_fit, near_pull, bridge_queries = call(
        functools.partial(own_near, features, share),
        (part, part, own_queries),
        (block, early_fit, fit_queries, own_operand, near_operand, *keys["near"]),
        10**9,
    )
    far_pull = call(
        functools.partial(own_far, features), part, (bridge_queries, *keys["far"]), 10**9
    )
    out = jax.ShapeDtypeStruct(noise.shape, f32)
    drift, moved = call(
        functools.partial(finish, features, share),
        (out, out),
        (block, noise, near_pull, far_pull, own_fit, *fits),
        10**6,
        out_spec=pl.BlockSpec(memory_space=pltpu.HBM),
        scratch=[
            pltpu.VMEM(noise.shape, f32),
            pltpu.VMEM(noise.shape, f32),
            pltpu.SemaphoreType.DMA((2,)),
        ],
    )
    return drift.transpose(1, 0, 2), moved.transpose(1, 0, 2)


def solution(mesh):
    in_specs = (
        P("tm", None, "particle"),
        P("tm", None, "cell"),
        P(),
        P("tm", None, ("particle", "cell")),
    )
    out_specs = (P("tm", None, ("particle", "cell")), P("tm", None, ("particle", "cell")))
    return jax.shard_map(shards, mesh=mesh, in_specs=in_specs, out_specs=out_specs, check_vma=False)
```
